32 devices in a mesh: ctx: 4 (over z), head: 4 (over x, core), grp: 2 (over y).
Axes of the slice: x: 2, y: 2, z: 4, core: 2. Of those that a mesh axis runs over, the one named last changes fastest.
Arguments:
- queries: bfloat16 [2, 256, 8192], P('grp', 'ctx', 'head'), may hold values from -40 to 40
- new_keys: bfloat16 [2, 256, 1024], P('grp', 'ctx', 'head'), may hold values from -40 to 40
- new_values: bfloat16 [2, 256, 1024], P('grp', 'ctx', 'head'), may hold values from -6 to 6
- page_keys: bfloat16 [2, 2048, 1024], P('grp', 'ctx', 'head'), may hold values from -6 to 6
- page_values: bfloat16 [2, 2048, 1024], P('grp', 'ctx', 'head'), may hold values from -6 to 6
- page_table: int32 [2, 1, 16], P('grp'), may hold values from 0 to 31, as said below
- page_slot: int32 [2, 32], P('grp'), may hold values from 0 to 31, each once within a row
- page_length: int32 [2, 32], P('grp'), may hold values from 1 to 64
Outputs:
- attended: bfloat16 [2, 256, 8192], P('grp', 'ctx', 'head')
The draws below stay inside these ranges and needn't reach their ends.
Inputs may be any that keep to these rules, and one draw needn't show every extreme that they name: `page_table`: the 16 page numbers of one request are distinct.
All inputs are finite; a program needn't handle non-finite values.
Results may differ from the reference program's by a relative error of at most 0.0055.
Values may be sent and summed in bfloat16 or wider, within the bound.
No kernel may reach another device: no remote copies, remote signals or barrier semaphores. Data moves between devices by JAX's collectives and lax.ppermute only.
A program may use at most 64 MiB of HBM per device.

```python
import math
import jax
import jax.numpy as jnp
from jax import lax

H = 64
KVH = 8
HD = 128
ROWS_DEV = 64
SPAN = 4
PAGE = 64
ROWS = 256
REQUESTS = 1
PAGES = 32
LIST = 16


def draw_new_keys(key, part):
    drawn = jax.random.truncated_normal(jax.random.fold_in(key, 12), -4.0, 4.0, (2, ROWS, KVH, HD), jnp.float32)
    return drawn.reshape(2, ROWS, KVH * HD).astype(jnp.bfloat16)


def draw_queries(key, part):
    drawn = 2.0 * jax.random.truncated_normal(jax.random.fold_in(key, 22), -4.0, 4.0, (2, ROWS, H, HD), jnp.float32)
    return drawn.reshape(2, ROWS, H * HD).astype(jnp.bfloat16)


def draw_page_table(key, part):
    subkeys = jax.random.split(jax.random.fold_in(key, 31), 2 * REQUESTS)

    def shuffled(single_key):
        return jax.random.permutation(single_key, PAGES)
    orders = jax.vmap(shuffled)(subkeys)
    return orders[:, :LIST].reshape(2, REQUESTS, LIST).astype(jnp.int32)


def touch_ends(array, key, low, top_value):
    spot = [jax.random.randint(jax.random.fold_in(key, axis), (), 0, length) for axis, length in enumerate(array.shape)]
    longest = array.shape.index(max(array.shape))
    beside = spot[:longest] + [(spot[longest] + 1) % array.shape[longest]] + spot[longest + 1:]
    return array.at[tuple(spot)].set(low).at[tuple(beside)].set(top_value)


def shard_levels(key, extent, shards, least, largest):
    factor_of, own = 1.0, jax.random.fold_in(key, 6)
    for axis_at, parts in shards:
        draws = jnp.exp(jax.random.uniform(jax.random.fold_in(own, axis_at), (parts,), jnp.float32, least / len(shards), largest / len(shards)))
        factor_of = factor_of * jnp.repeat(draws, extent[axis_at] // parts).reshape([-1 if axis == axis_at else 1 for axis in range(len(extent))])
    return factor_of


def scatter_about(stream_key, dims, width, reach, shards=(), kind=jnp.bfloat16):
    array = jax.random.normal(stream_key, dims, jnp.float32) * width
    if len(shards) > 0:
        array = shard_levels(stream_key, dims, shards, -0.22, 0.18) * array
    return jnp.clip(array, min=-reach, max=reach).astype(kind)


def setup_inputs(seed: int = 0) -> dict:
    arg_keys = jax.random.split(jax.random.key(seed), 9)
    queries = draw_queries(jax.random.fold_in(arg_keys[8], 71), 0)
    new_keys = draw_new_keys(jax.random.fold_in(arg_keys[8], 71), 0)
    new_values = scatter_about(arg_keys[2], (2, ROWS, KVH * HD), 1.0, 6.0, ((0, 2), (1, 4), (2, 4)))
    page_keys = scatter_about(arg_keys[3], (2, PAGES * PAGE, KVH * HD), 1.0, 6.0, ((0, 2), (1, 4), (2, 4)))
    page_values = scatter_about(arg_keys[4], (2, PAGES * PAGE, KVH * HD), 1.0, 6.0, ((0, 2), (1, 4), (2, 4)))
    page_table = draw_page_table(jax.random.fold_in(arg_keys[8], 71), 0)
    page_slot = jax.vmap(lambda own: jax.random.permutation(own, PAGES))(jax.random.split(arg_keys[6], 2)).reshape((2, PAGES)).astype(jnp.int32)
    page_length = touch_ends(jax.random.randint(arg_keys[7], (2, PAGES), 1, PAGE + 1), jax.random.fold_in(arg_keys[7], 1), 1, PAGE).astype(jnp.int32)
    return dict(queries=queries, new_keys=new_keys, new_values=new_values, page_keys=page_keys, page_values=page_values, page_table=page_table, page_slot=page_slot, page_length=page_length)


neg_floor = -1e+30

def pool_output(pool_index, queries, new_keys, new_values, page_keys, page_values, page_table, page_slot, page_length):
    request_rows = SPAN * ROWS_DEV
    requests = ROWS // request_rows
    group_size = H // KVH
    scaling = 1.0 / math.sqrt(HD)
    numbers = jnp.arange(PAGES, dtype=jnp.int32)
    listed = jnp.any(page_table[pool_index][:, :, None] == numbers[None, None, :], axis=1).astype(jnp.float32)
    placed = (page_slot[pool_index][:, None] == numbers[None, :]).astype(jnp.float32)
    listed_slot = jnp.dot(listed, placed, precision=lax.Precision.HIGHEST)
    length_slot = jnp.dot(page_length[pool_index].astype(jnp.float32), placed, precision=lax.Precision.HIGHEST)
    offsets = jnp.arange(PAGE, dtype=jnp.int32).astype(jnp.float32)
    page_open = (listed_slot[:, :, None] > 0.5) & (offsets[None, None, :] < length_slot[None, :, None])
    page_open = page_open.reshape(requests, PAGES * PAGE)
    cache_keys = page_keys[pool_index].astype(jnp.float32).reshape(PAGES * PAGE, KVH, HD)
    cache_values = page_values[pool_index].astype(jnp.float32).reshape(PAGES * PAGE, KVH, HD)
    positions = jnp.arange(request_rows, dtype=jnp.int32)
    causal = positions[:, None] >= positions[None, :]
    handed = jnp.full((request_rows, request_rows), pool_index == 1)

    def per_request(request_index):
        first_row = (request_index * request_rows).astype(jnp.int32)
        query_block = lax.dynamic_slice_in_dim(queries[pool_index], first_row, request_rows, 0)
        query_block = query_block.astype(jnp.float32).reshape(request_rows, KVH, group_size, HD)

        def rows_of(source):
            return lax.dynamic_slice_in_dim(source, first_row, request_rows, 0).astype(jnp.float32).reshape(request_rows, KVH, HD)
        all_keys = jnp.concatenate([cache_keys, rows_of(new_keys[pool_index]), rows_of(new_keys[0])], axis=0)
        all_values = jnp.concatenate([cache_values, rows_of(new_values[pool_index]), rows_of(new_values[0])], axis=0)
        page_row = lax.dynamic_index_in_dim(page_open, request_index, 0, keepdims=False)
        allowed = jnp.concatenate([jnp.broadcast_to(page_row[None, :], (request_rows, PAGES * PAGE)), causal, handed], axis=1)

        def per_head(head_index):
            query_head = lax.dynamic_index_in_dim(query_block, head_index, 1, keepdims=False)
            key_head = lax.dynamic_index_in_dim(all_keys, head_index, 1, keepdims=False)
            value_head = lax.dynamic_index_in_dim(all_values, head_index, 1, keepdims=False)
            scores = jnp.einsum('sgd,nd->gsn', query_head, key_head) * scaling
            masked = jnp.where(allowed[None], scores, neg_floor)
            row_max = lax.optimization_barrier(jnp.max(masked, axis=-1, keepdims=True))
            weights = jnp.where(allowed[None], jnp.exp(masked - row_max), 0.0)
            total = lax.optimization_barrier(jnp.sum(weights, axis=-1))
            rounded = weights.astype(jnp.bfloat16).astype(jnp.float32)
            numerator = jnp.einsum('gsn,nd->gsd', rounded, value_head)
            return numerator / total[..., None]
        per_heads = lax.map(per_head, jnp.arange(KVH, dtype=jnp.int32))
        return per_heads.transpose(2, 0, 1, 3).reshape(request_rows, H * HD)
    results = lax.map(per_request, jnp.arange(requests, dtype=jnp.int32))
    return results.reshape(ROWS, H * HD).astype(jnp.bfloat16)

def reference(queries, new_keys, new_values, page_keys, page_values, page_table, page_slot, page_length):
    prefill_part = pool_output(0, queries, new_keys, new_values, page_keys, page_values, page_table, page_slot, page_length)
    decode_part = pool_output(1, queries, new_keys, new_values, page_keys, page_values, page_table, page_slot, page_length)
    return jnp.stack([prefill_part, decode_part])
```

```python
import functools
import math

import jax
import jax.numpy as jnp
from jax import lax
from jax.experimental import pallas as pl
from jax.experimental.pallas import tpu as pltpu
from jax.sharding import PartitionSpec as P

HD = 128
SPAN = 4
PAGE = 64
CAP = 8

neg_floor = -1e30
far_limit = 1 << 30
log2_scale = math.log2(math.e) / math.sqrt(HD)

ANY = pl.BlockSpec(memory_space=pl.ANY)
VMEM = pl.BlockSpec(memory_space=pltpu.VMEM)
SMEM = pl.BlockSpec(memory_space=pltpu.SMEM)


def call(body, outs, in_specs, out_specs, scratch=(), flops=0, nbytes=0):
    return pl.pallas_call(
        body,
        out_shape=outs,
        in_specs=in_specs,
        out_specs=out_specs,
        scratch_shapes=scratch,
        compiler_params=pltpu.CompilerParams(vmem_limit_bytes=40 << 20),
        cost_estimate=pl.CostEstimate(flops=flops, bytes_accessed=nbytes, transcendentals=0),
    )


def sds(shape, dtype=jnp.bfloat16):
    return jax.ShapeDtypeStruct(shape, dtype)


def pack_body(
    table, slot, length, nk, nv, pk, pv, pack0, pack1, fresh, limits, source, count, sem, *, cap
):
    position = lax.axis_index("ctx")
    holders = lax.axis_size("ctx")
    held = slot.shape[1] // holders
    for i in range(holders * held):
        limits[i] = 0
        source[i] = 0
    for i in range(holders):
        count[i] = 0

    @pl.loop(0, table.shape[2])
    def _(i):
        number = table[0, 0, i]
        place = slot[0, number]
        holder = place // held
        nth = count[holder]
        count[holder] = nth + 1
        limits[holder * held + nth] = length[0, number]
        source[holder * held + nth] = place - holder * held

    copies = []
    for j in range(cap):
        first = pl.multiple_of(source[position * held + j] * PAGE, PAGE)
        for g, pack in enumerate((pack0, pack1)):
            for w, pages in enumerate((pk, pv)):
                copy = pltpu.make_async_copy(
                    pages.at[0, pl.ds(first, PAGE), pl.ds(g * HD, HD)],
                    pack.at[w, pl.ds(j * PAGE, PAGE), :],
                    sem.at[(j * 2 + g) * 2 + w],
                )
                copy.start()
                copies.append(copy)
    fresh[0] = nk[0]
    fresh[1] = nv[0]
    for copy in copies:
        copy.wait()


def holder_ids(position):
    left = position < 2
    return (
        position,
        position ^ 1,
        jnp.where(left, 2, 1),
        jnp.where(left, 3, 0),
    )


def is_inner(position):
    return (position == 1) | (position == 2)


def heads_of(ref, g, group):
    return jnp.concatenate(
        [ref[0, :, (g * group + i) * HD : (g * group + i + 1) * HD] for i in range(group)], axis=0
    )


def page_bias(limits, holder, held, cap):
    column = lax.broadcasted_iota(jnp.int32, (1, cap * PAGE), 1)
    page = column // PAGE
    within = column - page * PAGE
    limit = jnp.zeros((1, cap * PAGE), jnp.int32)
    for j in range(cap):
        limit = jnp.where(page == j, limits[holder * held + j], limit)
    return jnp.where(within < limit, 0.0, neg_floor).astype(jnp.float32)


def causal_bias(position, holder, rows, rows_dev):
    row = lax.broadcasted_iota(jnp.int32, (rows, rows_dev), 0) % rows_dev
    column = lax.broadcasted_iota(jnp.int32, (rows, rows_dev), 1)
    allowed = position * rows_dev + row >= holder * rows_dev + column
    return jnp.where(allowed, 0.0, neg_floor).astype(jnp.float32)


def scored(q, k, bias):
    s = lax.dot_general(q, k, (((1,), (1,)), ((), ())), preferred_element_type=jnp.float32)
    return s * log2_scale + bias


def attend(q, blocks, state=None):
    scores = [scored(q, k, bias) for k, _, bias in blocks]
    top = functools.reduce(jnp.maximum, [jnp.max(s, axis=1, keepdims=True) for s in scores])
    if state is not None:
        old_top, old_total, old_acc = state
        top = jnp.maximum(top, old_top)
        rescale = jnp.exp2(old_top - top)
    total = 0.0
    acc = 0.0
    for s, (_, v, _) in zip(scores, blocks):
        w = jnp.exp2(s - top)
        total = total + jnp.sum(w, axis=1, keepdims=True)
        acc = acc + jnp.dot(w.astype(jnp.bfloat16), v, preferred_element_type=jnp.float32)
    if state is not None:
        total = total + old_total * rescale
        acc = acc + old_acc * rescale
    return top, total, acc


def save_state(stats, accs, g, state):
    top, total, acc = state
    lane = lax.broadcasted_iota(jnp.int32, acc.shape, 1)
    stats[g] = jnp.where(lane == 0, top, total)
    accs[g] = acc


def load_state(stats, accs):
    return stats[0][:, 0:1], stats[0][:, 1:2], accs[0]


def first_body(
    limits, q, own0, own1, near0, near1, far0, far1, n_own, n_near, n_far, n_last, stats, accs,
    *, cap, shift
):
    position = lax.axis_index("ctx")
    held = limits.shape[0] // lax.axis_size("ctx")
    rows_dev = n_own.shape[1]
    group = q.shape[2] // HD // 2

    @pl.when(is_inner(position))
    def _():
        ids = holder_ids(position)
        target = position ^ shift
        biases = [page_bias(limits, ids[i], held, cap) for i in range(3)]
        causal = [causal_bias(target, i, group * rows_dev, rows_dev) for i in ids]
        fresh = jnp.concatenate(causal, axis=1)
        for g, packs in enumerate(((own0, near0, far0), (own1, near1, far1))):
            cols = slice(g * HD, (g + 1) * HD)
            blocks = [(p[0], p[1], b) for p, b in zip(packs, biases)]
            news = (n_own, n_near, n_far, n_last)
            nk = jnp.concatenate([n[0, :, cols] for n in news], axis=0)
            nv = jnp.concatenate([n[1, :, cols] for n in news], axis=0)
            blocks.append((nk, nv, fresh))
            save_state(stats, accs, g, attend(heads_of(q, g, group), blocks))


def last_body(
    limits, q_own, q_end, pack, taken, stats_own, acc_own, stats_end, acc_end, out_own, out_end,
    *, cap, g
):
    position = lax.axis_index("ctx")
    held = limits.shape[0] // lax.axis_size("ctx")
    rows_dev = q_own.shape[1]
    group = q_own.shape[2] // HD // 2

    @pl.when(is_inner(position))
    def _():
        ids = holder_ids(position)
        bias = page_bias(limits, ids[3], held, cap)
        cols = slice(g * HD, (g + 1) * HD)
        shut = jnp.where(lax.axis_index("grp") == 1, 0.0, neg_floor).astype(jnp.float32)
        tk = jnp.concatenate([taken[i, 0, :, cols] for i in range(taken.shape[0])], axis=0)
        tv = jnp.concatenate([taken[i, 1, :, cols] for i in range(taken.shape[0])], axis=0)
        blocks = [
            (pack[0], pack[1], bias),
            (tk, tv, jnp.full((1, tk.shape[0]), shut, jnp.float32)),
        ]
        for q, stats, acc, out in (
            (q_end, stats_end, acc_end, out_end),
            (q_own, stats_own, acc_own, out_own),
        ):
            state = stats[g][:, 0:1], stats[g][:, 1:2], acc[g]
            _, total, num = attend(heads_of(q, g, group), blocks, state)
            result = (num / total).astype(jnp.bfloat16)
            for i in range(group):
                out[:, i * HD : (i + 1) * HD] = result[i * rows_dev : (i + 1) * rows_dev]


def join_body(own0, own1, back0, back1, out):
    inner = is_inner(lax.axis_index("ctx"))
    half = own0.shape[1]

    @pl.when(inner)
    def _():
        out[0, :, :half] = own0[...]
        out[0, :, half:] = own1[...]

    @pl.when(jnp.logical_not(inner))
    def _():
        out[0, :, :half] = back0[...]
        out[0, :, half:] = back1[...]


def chain_local(
    queries, new_keys, new_values, page_keys, page_values, page_table, page_slot, page_length
):
    rows_dev = queries.shape[1]
    width = new_keys.shape[2]
    group = queries.shape[2] // width
    holders = lax.axis_size("ctx")
    heads = lax.axis_size("head")
    held = page_slot.shape[1] // holders
    cap = CAP
    keys = cap * PAGE
    side = [(i, i ^ 1) for i in range(holders)]
    middle = []
    for h in range(heads):
        other = h ^ 1 if h ^ 1 < heads else h
        for c in range(holders):
            if c in (1, 2):
                middle.append((c * heads + h, (3 - c) * heads + h))
            else:
                middle.append((c * heads + h, c * heads + other))

    def swap_side(x):
        return lax.ppermute(x, "ctx", side)

    def swap_middle(x):
        return lax.ppermute(x, ("ctx", "head"), middle)

    pack0, pack1, fresh, limits = call(
        functools.partial(pack_body, cap=cap),
        (
            sds((2, keys, HD)),
            sds((2, keys, HD)),
            sds((2, rows_dev, width)),
            sds((holders * held,), jnp.int32),
        ),
        [SMEM, SMEM, SMEM, VMEM, VMEM, ANY, ANY],
        (VMEM, VMEM, VMEM, SMEM),
        [
            pltpu.SMEM((holders * held,), jnp.int32),
            pltpu.SMEM((holders,), jnp.int32),
            pltpu.SemaphoreType.DMA((cap * 4,)),
        ],
        nbytes=2 << 20,
    )(page_table, page_slot, page_length, new_keys, new_values, page_keys, page_values)

    n_near = swap_side(fresh)
    n_far = swap_middle(fresh)
    near0 = swap_side(pack0)
    far0 = swap_middle(pack0)
    near1 = swap_side(pack1)
    far1 = swap_middle(pack1)
    q_end = swap_side(queries)
    n_last = swap_middle(n_near)
    last0 = swap_middle(near0)
    last1 = swap_middle(near1)
    taken = lax.ppermute(jnp.stack([fresh, n_near, n_far, n_last]), "grp", [(0, 1), (1, 0)])

    rows = group * rows_dev
    pair_flops = 4 * rows * HD
    state = (sds((2, rows, HD), jnp.float32), sds((2, rows, HD), jnp.float32))
    common = (pack0, pack1, near0, near1, far0, far1, fresh, n_near, n_far, n_last)

    def first(q, shift):
        return call(
            functools.partial(first_body, cap=cap, shift=shift),
            state,
            [SMEM] + [VMEM] * 11,
            (VMEM, VMEM),
            flops=2 * pair_flops * (3 * keys + 4 * rows_dev),
            nbytes=4 << 20,
        )(limits, q, *common)

    stats_own, acc_own = first(queries, 0)
    stats_end, acc_end = first(q_end, 1)

    def last(pack, g):
        return call(
            functools.partial(last_body, cap=cap, g=g),
            (sds((rows_dev, group * HD)), sds((rows_dev, group * HD))),
            [SMEM] + [VMEM] * 8,
            (VMEM, VMEM),
            flops=2 * pair_flops * (keys + 4 * rows_dev),
            nbytes=3 << 20,
        )(limits, queries, q_end, pack, taken, stats_own, acc_own, stats_end, acc_end)

    own0, end0 = last(last0, 0)
    back0 = swap_side(end0)
    own1, end1 = last(last1, 1)
    back1 = swap_side(end1)
    return call(join_body, sds(queries.shape), [VMEM] * 4, VMEM, nbytes=1 << 20)(
        own0, own1, back0, back1
    )


def passed_along(block, axis, distance):
    devices = range(lax.axis_size(axis))
    route = [(i - distance, i) for i in devices if i - distance in devices]
    return lax.ppermute(block, axis, route)


def passed_along_2(block, axis, distance):
    devices = range(lax.axis_size(axis))
    route = [((i - distance) % len(devices), i) for i in devices]
    return lax.ppermute(block, axis, route)


def ring_local(
    queries, new_keys, new_values, page_keys, page_values, page_table, page_slot, page_length
):
    query_rows = queries[0]
    rows_dev = query_rows.shape[0]
    key_width = new_keys.shape[2]
    shared_heads = key_width // HD
    query_count = query_rows.shape[1] // HD
    group_size = query_count // shared_heads
    scaling = 1.0 / math.sqrt(HD)
    position = lax.axis_index("ctx")
    cycle_size = lax.axis_size("ctx")
    pool_index = lax.axis_index("grp")
    request = position // SPAN
    row_ids = position * rows_dev + jnp.arange(rows_dev, dtype=jnp.int32)
    query_heads = query_rows.reshape(rows_dev, shared_heads, group_size, HD).transpose(1, 2, 0, 3)
    pages_total = page_slot.shape[1]
    numbers = jnp.arange(pages_total, dtype=jnp.int32)
    listed = jnp.any(page_table[0][:, :, None] == numbers[None, None, :], axis=1).astype(
        jnp.float32
    )
    own_listed = lax.dynamic_index_in_dim(listed, request, 0, keepdims=False)
    placed = (page_slot[0][:, None] == numbers[None, :]).astype(jnp.float32)
    listed_slot = jnp.dot(own_listed, placed, precision=lax.Precision.HIGHEST)
    length_slot = jnp.dot(
        page_length[0].astype(jnp.float32), placed, precision=lax.Precision.HIGHEST
    )
    offsets = jnp.arange(PAGE, dtype=jnp.int32).astype(jnp.float32)
    page_open = (listed_slot[:, None] > 0.5) & (offsets[None, :] < length_slot[:, None])
    page_limits = jnp.where(page_open, 0, far_limit).astype(jnp.int32).reshape(cycle_size, -1)

    def own_limits(holder):
        same = holder // SPAN == request
        return jnp.where(same, holder * rows_dev + jnp.arange(rows_dev, dtype=jnp.int32), far_limit)

    def taken_limits(holder):
        same = (holder // SPAN == request) & (pool_index == 1)
        return jnp.where(same, jnp.zeros((rows_dev,), jnp.int32), far_limit)

    def absorb_rows(carried, key_rows, value_rows, limits):
        maxima, totals, accumulated = carried
        pieces = key_rows.shape[0]
        key_heads = key_rows.reshape(pieces, shared_heads, HD)
        value_heads = value_rows.reshape(pieces, shared_heads, HD)
        scores = (
            jnp.einsum("kgrd,nkd->kgrn", query_heads, key_heads, preferred_element_type=jnp.float32)
            * scaling
        )
        allowed = row_ids[:, None] >= limits[None, :]
        masked = jnp.where(allowed, scores, neg_floor)
        new_max = jnp.maximum(maxima, jnp.max(masked, axis=-1))
        weights = jnp.where(allowed, jnp.exp(masked - new_max[..., None]), 0.0)
        rescale = jnp.exp(maxima - new_max)
        totals = totals * rescale + jnp.sum(weights, axis=-1)
        product = jnp.einsum(
            "kgrn,nkd->kgrd",
            weights.astype(jnp.bfloat16),
            value_heads,
            preferred_element_type=jnp.float32,
        )
        accumulated = accumulated * rescale[..., None] + product
        return (new_max, totals, accumulated)

    own_pairs = jnp.stack([new_keys[0], new_values[0]])
    taken_pairs = passed_along(own_pairs, "grp", 1)
    page_pairs = jnp.stack([page_keys[0], page_values[0]])
    carried = (
        jnp.full((shared_heads, group_size, rows_dev), neg_floor, jnp.float32),
        jnp.zeros((shared_heads, group_size, rows_dev), jnp.float32),
        jnp.zeros((shared_heads, group_size, rows_dev, HD), jnp.float32),
    )
    moving_rows = jnp.concatenate([page_pairs, own_pairs, taken_pairs], axis=1)

    def block_limits(holder):
        page_part = lax.dynamic_index_in_dim(page_limits, holder, 0, keepdims=False)
        return jnp.concatenate([page_part, own_limits(holder), taken_limits(holder)])

    def advance(stride, state_pair):
        inner, travelling = state_pair
        holder = (position - stride) % cycle_size
        inner = absorb_rows(inner, travelling[0], travelling[1], block_limits(holder))
        travelling = passed_along_2(travelling, "ctx", 1)
        return (inner, travelling)

    carried, moving_rows = lax.fori_loop(0, cycle_size - 1, advance, (carried, moving_rows))
    carried = absorb_rows(
        carried, moving_rows[0], moving_rows[1], block_limits((position + 1) % cycle_size)
    )
    maxima, totals, accumulated = carried
    attended = accumulated / totals[..., None]
    attended = attended.transpose(2, 0, 1, 3).reshape(rows_dev, query_count * HD)
    return attended.astype(jnp.bfloat16)[None]


def solution(mesh):
    in_specs = (
        P("grp", "ctx", "head"),
        P("grp", "ctx", "head"),
        P("grp", "ctx", "head"),
        P("grp", "ctx", "head"),
        P("grp", "ctx", "head"),
        P("grp", None, None),
        P("grp", None),
        P("grp", None),
    )
    chain = mesh.shape["ctx"] == SPAN == 4 and mesh.shape["grp"] == 2
    local = chain_local if chain else ring_local
    out_specs = P("grp", "ctx", "head")
    return jax.shard_map(local, mesh=mesh, in_specs=in_specs, out_specs=out_specs, check_vma=False)
```

```python
import functools
import math

import jax
import jax.numpy as jnp
from jax import lax
from jax.experimental import pallas as pl
from jax.experimental.pallas import tpu as pltpu
from jax.sharding import PartitionSpec as P


HD = 128
SPAN = 4
PAGE = 64
CAP = 8

neg_floor = -1e30
far_limit = 1 << 30
log2_scale = math.log2(math.e) / math.sqrt(HD)

HBM = pl.BlockSpec(memory_space=pltpu.HBM)
VMEM = pl.BlockSpec(memory_space=pltpu.VMEM)
SMEM = pl.BlockSpec(memory_space=pltpu.SMEM)


def call(body, outs, in_specs, out_specs, scratch=(), flops=0, nbytes=0):
    return pl.pallas_call(
        body,
        out_shape=outs,
        in_specs=in_specs,
        out_specs=out_specs,
        scratch_shapes=scratch,
        compiler_params=pltpu.CompilerParams(vmem_limit_bytes=40 << 20),
        cost_estimate=pl.CostEstimate(flops=flops, bytes_accessed=nbytes, transcendentals=0),
    )


def sds(shape, dtype=jnp.bfloat16):
    return jax.ShapeDtypeStruct(shape, dtype)


def ready_body(nk, nv, q, fresh, q0, q1, sem):
    half = q0.shape[1]
    copies = [
        pltpu.make_async_copy(nk.at[0], fresh.at[0], sem.at[0]),
        pltpu.make_async_copy(nv.at[0], fresh.at[1], sem.at[1]),
        pltpu.make_async_copy(q.at[0, :, pl.ds(0, half)], q0, sem.at[2]),
        pltpu.make_async_copy(q.at[0, :, pl.ds(half, half)], q1, sem.at[3]),
    ]
    for copy in copies:
        copy.start()
    for copy in copies:
        copy.wait()


def pack_body(
    table_in, slot_in, length_in, pk, pv, pack0, pack1, limits, table, slot, length, source, count,
    sem, *, cap
):
    position = lax.axis_index("ctx")
    holders = lax.axis_size("ctx")
    held = slot.shape[1] // holders
    reads = [
        pltpu.make_async_copy(table_in, table, sem.at[0]),
        pltpu.make_async_copy(slot_in, slot, sem.at[1]),
        pltpu.make_async_copy(length_in, length, sem.at[2]),
    ]
    for copy in reads:
        copy.start()
    for i in range(holders * held):
        limits[i] = 0
        source[i] = 0
    for i in range(holders):
        count[i] = 0
    for copy in reads:
        copy.wait()
    for i in range(table.shape[2]):
        number = table[0, 0, i]
        place = slot[0, number]
        holder = place // held
        nth = count[holder]
        count[holder] = nth + 1
        limits[holder * held + nth] = length[0, number]
        source[holder * held + nth] = place - holder * held

    copies = []
    for g, pack in enumerate((pack0, pack1)):
        for j in range(cap):
            first = pl.multiple_of(source[position * held + j] * PAGE, PAGE)
            for w, pages in enumerate((pk, pv)):
                copy = pltpu.make_async_copy(
                    pages.at[0, pl.ds(first, PAGE), pl.ds(g * HD, HD)],
                    pack.at[w, pl.ds(j * PAGE, PAGE), :],
                    sem.at[(j * 2 + g) * 2 + w],
                )
                copy.start()
                copies.append(copy)
    for copy in copies:
        copy.wait()


def holder_ids(position):
    left = position < 2
    return (
        position,
        position ^ 1,
        jnp.where(left, 2, 1),
        jnp.where(left, 3, 0),
    )


def is_inner(position):
    return (position == 1) | (position == 2)


def heads_of(ref):
    return jnp.concatenate(
        [ref[:, i * HD : (i + 1) * HD] for i in range(ref.shape[1] // HD)], axis=0
    )


def page_bias(limits, holder, held, cap):
    column = lax.broadcasted_iota(jnp.int32, (1, cap * PAGE), 1)
    page = column // PAGE
    within = column - page * PAGE
    limit = jnp.zeros((1, cap * PAGE), jnp.int32)
    for j in range(cap):
        limit = jnp.where(page == j, limits[holder * held + j], limit)
    return jnp.where(within < limit, 0.0, neg_floor).astype(jnp.float32)


def causal_bias(position, holder, rows, rows_dev):
    row = lax.broadcasted_iota(jnp.int32, (rows, rows_dev), 0) % rows_dev
    column = lax.broadcasted_iota(jnp.int32, (rows, rows_dev), 1)
    allowed = position * rows_dev + row >= holder * rows_dev + column
    return jnp.where(allowed, 0.0, neg_floor).astype(jnp.float32)


def scored(q, k, bias):
    s = lax.dot_general(q, k, (((1,), (1,)), ((), ())), preferred_element_type=jnp.float32)
    return s * log2_scale + bias


def attend(q, blocks, state=None):
    scores = [scored(q, k, bias) for k, _, bias in blocks]
    shape = (q.shape[0], HD)
    top = functools.reduce(jnp.maximum, [jnp.max(s, axis=1, keepdims=True) for s in scores])
    if state is not None:
        old_top, old_total, old_acc = state
        wide = jnp.maximum(jnp.broadcast_to(top, shape), old_top)
        rescale = jnp.exp2(old_top - wide)
        top = wide[:, 0:1]
    total = 0.0
    acc = 0.0
    for s, (_, v, _) in zip(scores, blocks):
        w = jnp.exp2(s - top)
        total = total + jnp.sum(w, axis=1, keepdims=True)
        acc = acc + jnp.dot(w.astype(jnp.bfloat16), v, preferred_element_type=jnp.float32)
    if state is None:
        return top, total, acc
    total = jnp.broadcast_to(total, shape) + old_total * rescale
    return total, acc + old_acc * rescale


def early_body(
    limits, q_own, q_end, own, near, far, n_own, n_near, n_far, n_last, tops, totals, accs, *, cap, g
):
    position = lax.axis_index("ctx")
    held = limits.shape[0] // lax.axis_size("ctx")
    rows_dev = n_own.shape[1]
    rows = accs.shape[1]

    @pl.when(is_inner(position))
    def _():
        ids = holder_ids(position)
        cols = slice(g * HD, (g + 1) * HD)
        news = (n_own, n_near, n_far, n_last)
        nk = jnp.concatenate([n[0, :, cols] for n in news], axis=0)
        nv = jnp.concatenate([n[1, :, cols] for n in news], axis=0)
        paged = [
            (p[0], p[1], page_bias(limits, i, held, cap)) for p, i in zip((own, near, far), ids)
        ]
        for t, q in enumerate((q_own, q_end)):
            causal = [causal_bias(position ^ t, i, rows, rows_dev) for i in ids]
            fresh = (nk, nv, jnp.concatenate(causal, axis=1))
            top, total, acc = attend(heads_of(q), paged + [fresh])
            tops[t] = jnp.broadcast_to(top, acc.shape)
            totals[t] = jnp.broadcast_to(total, acc.shape)
            accs[t] = acc


def late_body(
    limits, q_own, q_end, pack, taken, tops, totals, accs, out_own, out_end, *, cap, g
):
    position = lax.axis_index("ctx")
    held = limits.shape[0] // lax.axis_size("ctx")
    rows_dev = q_own.shape[0]

    @pl.when(is_inner(position))
    def _():
        ids = holder_ids(position)
        cols = slice(g * HD, (g + 1) * HD)
        shut = jnp.where(lax.axis_index("grp") == 1, 0.0, neg_floor).astype(jnp.float32)
        tk = jnp.concatenate([taken[i, 0, :, cols] for i in range(taken.shape[0])], axis=0)
        tv = jnp.concatenate([taken[i, 1, :, cols] for i in range(taken.shape[0])], axis=0)
        blocks = [
            (pack[0], pack[1], page_bias(limits, ids[3], held, cap)),
            (tk, tv, jnp.full((1, tk.shape[0]), shut, jnp.float32)),
        ]
        for t, q, out in ((1, q_end, out_end), (0, q_own, out_own)):
            total, num = attend(heads_of(q), blocks, (tops[t], totals[t], accs[t]))
            result = (num / total).astype(jnp.bfloat16)
            for i in range(out.shape[1] // HD):
                out[:, i * HD : (i + 1) * HD] = result[i * rows_dev : (i + 1) * rows_dev]


def join_body(own0, own1, back0, back1, out):
    inner = is_inner(lax.axis_index("ctx"))
    half = own0.shape[1]

    @pl.when(inner)
    def _():
        out[0, :, :half] = own0[...]
        out[0, :, half:] = own1[...]

    @pl.when(jnp.logical_not(inner))
    def _():
        out[0, :, :half] = back0[...]
        out[0, :, half:] = back1[...]


def chain_local(*args):
    return chain_steps(*args)


def chain_steps(
    queries, new_keys, new_values, page_keys, page_values, page_table, page_slot, page_length
):
    rows_dev = queries.shape[1]
    width = new_keys.shape[2]
    group = queries.shape[2] // width
    holders = lax.axis_size("ctx")
    heads = lax.axis_size("head")
    held = page_slot.shape[1] // holders
    cap = CAP
    keys = cap * PAGE
    side = [(i, i ^ 1) for i in range(holders)]
    middle = []
    for h in range(heads):
        other = h ^ 1 if h ^ 1 < heads else h
        for c in range(holders):
            if c in (1, 2):
                middle.append((c * heads + h, (3 - c) * heads + h))
            else:
                middle.append((c * heads + h, c * heads + other))

    def swap_side(x):
        return lax.ppermute(x, "ctx", side)

    def swap_middle(x):
        return lax.ppermute(x, ("ctx", "head"), middle)

    def swap_pools(x):
        return lax.ppermute(x, "grp", [(0, 1), (1, 0)])

    half = sds((rows_dev, group * HD))
    fresh, q0, q1 = call(
        ready_body,
        (sds((2, rows_dev, width)), half, half),
        [HBM] * 3,
        (VMEM,) * 3,
        [pltpu.SemaphoreType.DMA((4,))],
        nbytes=1 << 20,
    )(new_keys, new_values, queries)
    pack0, pack1, limits = call(
        functools.partial(pack_body, cap=cap),
        (sds((2, keys, HD)), sds((2, keys, HD)), sds((holders * held,), jnp.int32)),
        [HBM] * 5,
        (VMEM, VMEM, SMEM),
        [
            pltpu.SMEM(page_table.shape, jnp.int32),
            pltpu.SMEM(page_slot.shape, jnp.int32),
            pltpu.SMEM(page_length.shape, jnp.int32),
            pltpu.SMEM((holders * held,), jnp.int32),
            pltpu.SMEM((holders,), jnp.int32),
            pltpu.SemaphoreType.DMA((cap * 4,)),
        ],
        nbytes=2 << 20,
    )(page_table, page_slot, page_length, page_keys, page_values)

    n_near = swap_side(fresh)
    n_far = swap_middle(fresh)
    q0_end = swap_side(q0)
    near0 = swap_side(pack0)
    far0 = swap_middle(pack0)
    n_last = swap_middle(n_near)
    near1 = swap_side(pack1)
    far1 = swap_middle(pack1)
    q1_end = swap_side(q1)
    taken = swap_pools(jnp.stack([fresh, n_near, n_far, n_last]))
    last0 = swap_middle(near0)
    last1 = swap_middle(near1)

    rows = group * rows_dev
    pair_flops = 4 * rows * HD
    state = (sds((2, rows, HD), jnp.float32),) * 3

    def early(g, q, q_end, own, near, far):
        return call(
            functools.partial(early_body, cap=cap, g=g),
            state,
            [SMEM] + [VMEM] * 9,
            (VMEM,) * 3,
            flops=2 * pair_flops * (3 * keys + 4 * rows_dev),
            nbytes=4 << 20,
        )(limits, q, q_end, own, near, far, fresh, n_near, n_far, n_last)

    def late(g, q, q_end, pack, carried):
        return call(
            functools.partial(late_body, cap=cap, g=g),
            (half, half),
            [SMEM] + [VMEM] * 7,
            (VMEM, VMEM),
            flops=2 * pair_flops * (keys + 4 * rows_dev),
            nbytes=3 << 20,
        )(limits, q, q_end, pack, taken, *carried)

    carried0 = early(0, q0, q0_end, pack0, near0, far0)
    carried1 = early(1, q1, q1_end, pack1, near1, far1)
    own0, end0 = late(0, q0, q0_end, last0, carried0)
    back0 = swap_side(end0)
    own1, end1 = late(1, q1, q1_end, last1, carried1)
    back1 = swap_side(end1)
    return call(join_body, sds(queries.shape), [VMEM] * 4, VMEM, nbytes=1 << 20)(
        own0, own1, back0, back1
    )


def passed_along(block, axis, distance):
    devices = range(lax.axis_size(axis))
    route = [(i - distance, i) for i in devices if i - distance in devices]
    return lax.ppermute(block, axis, route)


def passed_along_2(block, axis, distance):
    devices = range(lax.axis_size(axis))
    route = [((i - distance) % len(devices), i) for i in devices]
    return lax.ppermute(block, axis, route)


def ring_local(
    queries, new_keys, new_values, page_keys, page_values, page_table, page_slot, page_length
):
    query_rows = queries[0]
    rows_dev = query_rows.shape[0]
    key_width = new_keys.shape[2]
    shared_heads = key_width // HD
    query_count = query_rows.shape[1] // HD
    group_size = query_count // shared_heads
    scaling = 1.0 / math.sqrt(HD)
    position = lax.axis_index("ctx")
    cycle_size = lax.axis_size("ctx")
    pool_index = lax.axis_index("grp")
    request = position // SPAN
    row_ids = position * rows_dev + jnp.arange(rows_dev, dtype=jnp.int32)
    query_heads = query_rows.reshape(rows_dev, shared_heads, group_size, HD).transpose(1, 2, 0, 3)
    pages_total = page_slot.shape[1]
    numbers = jnp.arange(pages_total, dtype=jnp.int32)
    listed = jnp.any(page_table[0][:, :, None] == numbers[None, None, :], axis=1).astype(
        jnp.float32
    )
    own_listed = lax.dynamic_index_in_dim(listed, request, 0, keepdims=False)
    placed = (page_slot[0][:, None] == numbers[None, :]).astype(jnp.float32)
    listed_slot = jnp.dot(own_listed, placed, precision=lax.Precision.HIGHEST)
    length_slot = jnp.dot(
        page_length[0].astype(jnp.float32), placed, precision=lax.Precision.HIGHEST
    )
    offsets = jnp.arange(PAGE, dtype=jnp.int32).astype(jnp.float32)
    page_open = (listed_slot[:, None] > 0.5) & (offsets[None, :] < length_slot[:, None])
    page_limits = jnp.where(page_open, 0, far_limit).astype(jnp.int32).reshape(cycle_size, -1)

    def own_limits(holder):
        same = holder // SPAN == request
        return jnp.where(same, holder * rows_dev + jnp.arange(rows_dev, dtype=jnp.int32), far_limit)

    def taken_limits(holder):
        same = (holder // SPAN == request) & (pool_index == 1)
        return jnp.where(same, jnp.zeros((rows_dev,), jnp.int32), far_limit)

    def absorb_rows(carried, key_rows, value_rows, limits):
        maxima, totals, accumulated = carried
        pieces = key_rows.shape[0]
        key_heads = key_rows.reshape(pieces, shared_heads, HD)
        value_heads = value_rows.reshape(pieces, shared_heads, HD)
        scores = (
            jnp.einsum("kgrd,nkd->kgrn", query_heads, key_heads, preferred_element_type=jnp.float32)
            * scaling
        )
        allowed = row_ids[:, None] >= limits[None, :]
        masked = jnp.where(allowed, scores, neg_floor)
        new_max = jnp.maximum(maxima, jnp.max(masked, axis=-1))
        weights = jnp.where(allowed, jnp.exp(masked - new_max[..., None]), 0.0)
        rescale = jnp.exp(maxima - new_max)
        totals = totals * rescale + jnp.sum(weights, axis=-1)
        product = jnp.einsum(
            "kgrn,nkd->kgrd",
            weights.astype(jnp.bfloat16),
            value_heads,
            preferred_element_type=jnp.float32,
        )
        accumulated = accumulated * rescale[..., None] + product
        return (new_max, totals, accumulated)

    own_pairs = jnp.stack([new_keys[0], new_values[0]])
    taken_pairs = passed_along(own_pairs, "grp", 1)
    page_pairs = jnp.stack([page_keys[0], page_values[0]])
    carried = (
        jnp.full((shared_heads, group_size, rows_dev), neg_floor, jnp.float32),
        jnp.zeros((shared_heads, group_size, rows_dev), jnp.float32),
        jnp.zeros((shared_heads, group_size, rows_dev, HD), jnp.float32),
    )
    moving_rows = jnp.concatenate([page_pairs, own_pairs, taken_pairs], axis=1)

    def block_limits(holder):
        page_part = lax.dynamic_index_in_dim(page_limits, holder, 0, keepdims=False)
        return jnp.concatenate([page_part, own_limits(holder), taken_limits(holder)])

    def advance(stride, state_pair):
        inner, travelling = state_pair
        holder = (position - stride) % cycle_size
        inner = absorb_rows(inner, travelling[0], travelling[1], block_limits(holder))
        travelling = passed_along_2(travelling, "ctx", 1)
        return (inner, travelling)

    carried, moving_rows = lax.fori_loop(0, cycle_size - 1, advance, (carried, moving_rows))
    carried = absorb_rows(
        carried, moving_rows[0], moving_rows[1], block_limits((position + 1) % cycle_size)
    )
    _, totals, accumulated = carried
    attended = accumulated / totals[..., None]
    attended = attended.transpose(2, 0, 1, 3).reshape(rows_dev, query_count * HD)
    return attended.astype(jnp.bfloat16)[None]


def solution(mesh):
    in_specs = (
        P("grp", "ctx", "head"),
        P("grp", "ctx", "head"),
        P("grp", "ctx", "head"),
        P("grp", "ctx", "head"),
        P("grp", "ctx", "head"),
        P("grp", None, None),
        P("grp", None),
        P("grp", None),
    )
    chain = mesh.shape["ctx"] == SPAN == 4 and mesh.shape["grp"] == 2
    local = chain_local if chain else ring_local
    out_specs = P("grp", "ctx", "head")
    return jax.shard_map(local, mesh=mesh, in_specs=in_specs, out_specs=out_specs, check_vma=False)
```

```python
import functools
import math

import jax
import jax.numpy as jnp
from jax import lax
from jax.experimental import pallas as pl
from jax.experimental.pallas import tpu as pltpu
from jax.sharding import PartitionSpec as P


HD = 128
SPAN = 4
PAGE = 64
CAP = 6


neg_floor = -1e30
far_limit = 1 << 30
log2_scale = math.log2(math.e) / math.sqrt(HD)

HBM = pl.BlockSpec(memory_space=pltpu.HBM)
VMEM = pl.BlockSpec(memory_space=pltpu.VMEM)
SMEM = pl.BlockSpec(memory_space=pltpu.SMEM)


def call(body, outs, in_specs, out_specs, scratch=(), flops=0, nbytes=0):
    return pl.pallas_call(
        body,
        out_shape=outs,
        in_specs=in_specs,
        out_specs=out_specs,
        scratch_shapes=scratch,
        compiler_params=pltpu.CompilerParams(vmem_limit_bytes=40 << 20),
        cost_estimate=pl.CostEstimate(flops=flops, bytes_accessed=nbytes, transcendentals=0),
    )


def sds(shape, dtype=jnp.bfloat16):
    return jax.ShapeDtypeStruct(shape, dtype)


def listed_pages(tables, places, limits, source, count, most, sem):
    table, slot, length = places
    holders = lax.axis_size("ctx")
    held = slot.shape[1] // holders
    reads = [
        pltpu.make_async_copy(wide, near, sem.at[i])
        for i, (wide, near) in enumerate(zip(tables, places))
    ]
    for copy in reads:
        copy.start()
    for i in range(holders * held):
        limits[i] = 0
        source[i] = 0
    for i in range(holders):
        count[i] = 0
    for copy in reads:
        copy.wait()
    for i in range(table.shape[2]):
        number = table[0, 0, i]
        place = slot[0, number]
        holder = place // held
        nth = count[holder]
        count[holder] = nth + 1
        limits[holder * held + nth] = length[0, number]
        source[holder * held + nth] = place - holder * held
    most[0] = functools.reduce(jnp.maximum, [count[i] for i in range(holders)])


def page_copies(packs, pages, source, first, cap, sem):
    position = lax.axis_index("ctx")
    held = source.shape[0] // lax.axis_size("ctx")
    copies = []
    for g, pack in enumerate(packs):
        for j in range(cap):
            row = pl.multiple_of(source[position * held + first + j] * PAGE, PAGE)
            for w, wide in enumerate(pages):
                copy = pltpu.make_async_copy(
                    wide.at[0, pl.ds(row, PAGE), pl.ds(g * HD, HD)],
                    pack.at[w, pl.ds(j * PAGE, PAGE), :],
                    sem.at[(j * 2 + g) * 2 + w],
                )
                copy.start()
                copies.append(copy)
    return copies


def pack_body(
    table_in, slot_in, length_in, pk, pv, nk, nv, q, pack0, pack1, q0, q1, limits, most,
    table, slot, length, source, count, sem, sem_new, *, cap
):
    half = q0.shape[1]
    rows_dev = nk.shape[1]
    copies = []
    for i, (wide, near) in enumerate(((0, q0), (half, q1))):
        copies.append(pltpu.make_async_copy(q.at[0, :, pl.ds(wide, half)], near, sem_new.at[i]))
    for w, new in enumerate((nk, nv)):
        for g in range(2):
            copies.append(
                pltpu.make_async_copy(
                    new.at[0, :, pl.ds(g * HD, HD)],
                    pack0.at[w, pl.ds(cap * PAGE + g * rows_dev, rows_dev), :],
                    sem_new.at[2 + w * 2 + g],
                )
            )
    for copy in copies:
        copy.start()
    listed_pages(
        (table_in, slot_in, length_in), (table, slot, length), limits, source, count, most, sem
    )
    copies += page_copies((pack0, pack1), (pk, pv), source, 0, cap, sem)
    for copy in copies:
        copy.wait()


def spare_body(
    table_in, slot_in, length_in, pk, pv, rest, table, slot, length, source, count, limits, most,
    sem, *, first, cap
):
    listed_pages(
        (table_in, slot_in, length_in), (table, slot, length), limits, source, count, most, sem
    )
    for copy in page_copies((rest.at[0], rest.at[1]), (pk, pv), source, first, cap, sem):
        copy.wait()


def blank_body(*refs):
    pass


def holder_ids(position):
    left = position < 2
    return (
        position,
        position ^ 1,
        jnp.where(left, 2, 1),
        jnp.where(left, 3, 0),
    )


def is_inner(position):
    return (position == 1) | (position == 2)


def heads_of(ref):
    return jnp.concatenate(
        [ref[:, i * HD : (i + 1) * HD] for i in range(ref.shape[1] // HD)], axis=0
    )


def page_bias(limits, holder, held, first, cap):
    column = lax.broadcasted_iota(jnp.int32, (1, cap * PAGE), 1)
    page = column // PAGE
    within = column - page * PAGE
    limit = jnp.zeros((1, cap * PAGE), jnp.int32)
    for j in range(cap):
        limit = jnp.where(page == j, limits[holder * held + first + j], limit)
    return jnp.where(within < limit, 0.0, neg_floor).astype(jnp.float32)


def causal_bias(position, ids, rows, rows_dev):
    shape = (rows_dev, len(ids) * rows_dev)
    row = lax.broadcasted_iota(jnp.int32, shape, 0)
    column = lax.broadcasted_iota(jnp.int32, (1, shape[1]), 1)
    key = jnp.zeros_like(column)
    for i, holder in enumerate(ids):
        key = jnp.where(column // rows_dev == i, column + (holder - i) * rows_dev, key)
    allowed = position * rows_dev + row >= key
    bias = jnp.where(allowed, 0.0, neg_floor).astype(jnp.float32)
    return jnp.concatenate([bias] * (rows // rows_dev), axis=0)


def scored(q, k, bias):
    s = lax.dot_general(q, k, (((1,), (1,)), ((), ())), preferred_element_type=jnp.float32)
    return s * log2_scale + bias


def attend(q, blocks, state=None):
    scores = [scored(q, k, bias) for k, _, bias in blocks]
    shape = (q.shape[0], HD)
    top = functools.reduce(jnp.maximum, [jnp.max(s, axis=1, keepdims=True) for s in scores])
    if state is not None:
        old_top, old_total, old_acc = state
        wide = jnp.maximum(jnp.broadcast_to(top, shape), old_top)
        rescale = jnp.exp2(old_top - wide)
        top = wide[:, 0:1]
    total = 0.0
    acc = 0.0
    for s, (_, v, _) in zip(scores, blocks):
        w = jnp.exp2(s - top)
        total = total + jnp.sum(w, axis=1, keepdims=True)
        acc = acc + jnp.dot(w.astype(jnp.bfloat16), v, preferred_element_type=jnp.float32)
    if state is None:
        return top, total, acc
    total = jnp.broadcast_to(total, shape) + old_total * rescale
    return total, acc + old_acc * rescale


def early_body(limits, q_own, q_end, *refs, cap, g):
    packs = refs[:3]
    news = refs[3:7] if len(refs) == 10 else packs + refs[3:4]
    tops, totals, accs = refs[-3:]
    position = lax.axis_index("ctx")
    held = limits.shape[0] // lax.axis_size("ctx")
    rows_dev = q_own.shape[0]
    rows = accs.shape[1]
    pages = cap * PAGE

    @pl.when(is_inner(position))
    def _():
        ids = holder_ids(position)
        firsts = [n.shape[1] - 2 * rows_dev + g * rows_dev for n in news]
        nk = jnp.concatenate([n[0, i : i + rows_dev] for n, i in zip(news, firsts)], axis=0)
        nv = jnp.concatenate([n[1, i : i + rows_dev] for n, i in zip(news, firsts)], axis=0)
        paged = [
            (p[0, :pages], p[1, :pages], page_bias(limits, i, held, 0, cap))
            for p, i in zip(packs, ids)
        ]
        for t, q in enumerate((q_own, q_end)):
            fresh = (nk, nv, causal_bias(position ^ t, ids, rows, rows_dev))
            top, total, acc = attend(heads_of(q), paged + [fresh])
            tops[t] = jnp.broadcast_to(top, acc.shape)
            totals[t] = jnp.broadcast_to(total, acc.shape)
            accs[t] = acc


def late_body(*refs, cap, g, tasks):
    n = len(tasks)
    limits, most = refs[:2]
    queries = refs[2 : 2 + n]
    pack, taken, tops, totals, accs = refs[2 + n : 7 + n]
    spilled = refs[7 + n : 11 + n]
    outs = refs[11 + n : 11 + 2 * n]
    extra, sem = refs[11 + 2 * n :]
    position = lax.axis_index("ctx")
    held = limits.shape[0] // lax.axis_size("ctx")

    def finish(more):
        ids = holder_ids(position)
        rows_dev = queries[0].shape[0]
        new = slice(g * rows_dev, (g + 1) * rows_dev)
        shut = jnp.where(lax.axis_index("grp") == 1, 0.0, neg_floor).astype(jnp.float32)
        tk = jnp.concatenate([taken[i, 0, new] for i in range(taken.shape[0])], axis=0)
        tv = jnp.concatenate([taken[i, 1, new] for i in range(taken.shape[0])], axis=0)
        blocks = [
            (pack[0], pack[1], page_bias(limits, ids[3], held, 0, cap)),
            (tk, tv, jnp.full((1, tk.shape[0]), shut, jnp.float32)),
        ]
        if more:
            copies = [
                pltpu.make_async_copy(ref.at[g], extra.at[i], sem.at[i])
                for i, ref in enumerate(spilled)
            ]
            for copy in copies:
                copy.start()
            for copy in copies:
                copy.wait()
            for i, holder in enumerate(ids):
                bias = page_bias(limits, holder, held, cap, held - cap)
                blocks.append((extra[i, 0], extra[i, 1], bias))
        for t, q, out in zip(tasks, queries, outs):
            total, num = attend(heads_of(q), blocks, (tops[t], totals[t], accs[t]))
            result = (num / total).astype(jnp.bfloat16)
            for i in range(out.shape[1] // HD):
                out[:, i * HD : (i + 1) * HD] = result[i * rows_dev : (i + 1) * rows_dev]

    inner = is_inner(position)
    over = most[0] > cap

    @pl.when(inner & jnp.logical_not(over))
    def _():
        finish(False)

    @pl.when(inner & over)
    def _():
        finish(True)


def join_body(own0, own1, back0, back1, out):
    inner = is_inner(lax.axis_index("ctx"))
    half = own0.shape[1]

    @pl.when(inner)
    def _():
        out[0, :, :half] = own0[...]
        out[0, :, half:] = own1[...]

    @pl.when(jnp.logical_not(inner))
    def _():
        out[0, :, :half] = back0[...]
        out[0, :, half:] = back1[...]


def chain_local(*args):
    return chain_steps(*args)


def chain_steps(
    queries, new_keys, new_values, page_keys, page_values, page_table, page_slot, page_length
):
    rows_dev = queries.shape[1]
    width = new_keys.shape[2]
    group = queries.shape[2] // width
    holders = lax.axis_size("ctx")
    heads = lax.axis_size("head")
    held = page_slot.shape[1] // holders
    cap = CAP
    keys = cap * PAGE
    side = [(i, i ^ 1) for i in range(holders)]
    middle = []
    for h in range(heads):
        other = h ^ 1 if h ^ 1 < heads else h
        for c in range(holders):
            if c in (1, 2):
                middle.append((c * heads + h, (3 - c) * heads + h))
            else:
                middle.append((c * heads + h, c * heads + other))

    def swap_side(x):
        return lax.ppermute(x, "ctx", side)

    def swap_middle(x):
        return lax.ppermute(x, ("ctx", "head"), middle)

    def swap_pools(x):
        return lax.ppermute(x, "grp", [(0, 1), (1, 0)])

    new_keys, new_values, queries, page_table, page_slot, page_length, page_keys, page_values = [
        pltpu.with_memory_space_constraint(x, pltpu.HBM)
        for x in (
            new_keys, new_values, queries, page_table, page_slot, page_length, page_keys,
            page_values,
        )
    ]
    half = sds((rows_dev, group * HD))
    tables = (page_table, page_slot, page_length, page_keys, page_values)
    scalars = [
        pltpu.SMEM(page_table.shape, jnp.int32),
        pltpu.SMEM(page_slot.shape, jnp.int32),
        pltpu.SMEM(page_length.shape, jnp.int32),
        pltpu.SMEM((holders * held,), jnp.int32),
        pltpu.SMEM((holders,), jnp.int32),
    ]
    pack0, pack1, q0, q1, limits, most = call(
        functools.partial(pack_body, cap=cap),
        (
            sds((2, keys + 2 * rows_dev, HD)),
            sds((2, keys, HD)),
            half,
            half,
            sds((holders * held,), jnp.int32),
            sds((1,), jnp.int32),
        ),
        [HBM] * 8,
        (VMEM, VMEM, VMEM, VMEM, SMEM, SMEM),
        scalars + [pltpu.SemaphoreType.DMA((cap * 4,)), pltpu.SemaphoreType.DMA((6,))],
        nbytes=3 << 20,
    )(*tables, new_keys, new_values, queries)

    near0 = swap_side(pack0)
    far0 = swap_middle(pack0)
    q0_end = swap_side(q0)
    n_last = swap_middle(near0[:, keys:])
    near1 = swap_side(pack1)
    far1 = swap_middle(pack1)
    q1_end = swap_side(q1)
    last0 = swap_middle(near0[:, :keys])
    fresh = [pack0[:, keys:], near0[:, keys:], far0[:, keys:], n_last]
    taken = swap_pools(jnp.stack(fresh))
    last1 = swap_middle(near1)
    spare = sds((2, 2, (held - cap) * PAGE, HD))

    def fetch():
        rest = call(
            functools.partial(spare_body, first=cap, cap=held - cap),
            spare,
            [HBM] * 5,
            VMEM,
            scalars
            + [
                pltpu.SMEM((holders * held,), jnp.int32),
                pltpu.SMEM((1,), jnp.int32),
                pltpu.SemaphoreType.DMA((max(held - cap, 1) * 4,)),
            ],
            nbytes=1 << 20,
        )(*tables)
        near = swap_side(rest)
        far = swap_middle(rest)
        return rest, near, far, swap_middle(near)

    def skip():
        return tuple(call(blank_body, (spare,) * 4, [], (HBM,) * 4)())

    spilled = lax.cond(most[0] > cap, fetch, skip)

    rows = group * rows_dev
    pair_flops = 4 * rows * HD
    state = (sds((2, rows, HD), jnp.float32),) * 3

    def early(g, q, q_end, packs, news):
        return call(
            functools.partial(early_body, cap=cap, g=g),
            state,
            [SMEM] + [VMEM] * (5 + len(news)),
            (VMEM,) * 3,
            flops=2 * pair_flops * (3 * keys + 4 * rows_dev),
            nbytes=4 << 20,
        )(limits, q, q_end, *packs, *news)

    def late(g, tasks, queries, pack, carried):
        return call(
            functools.partial(late_body, cap=cap, g=g, tasks=tasks),
            (half,) * len(tasks),
            [SMEM, SMEM] + [VMEM] * (5 + len(tasks)) + [HBM] * 4,
            (VMEM,) * len(tasks),
            [pltpu.VMEM((4, 2, (held - cap) * PAGE, HD), jnp.bfloat16), pltpu.SemaphoreType.DMA((4,))],
            flops=len(tasks) * pair_flops * (keys + 4 * rows_dev),
            nbytes=len(tasks) << 20,
        )(limits, most, *queries, pack, taken, *carried, *spilled)

    carried0 = early(0, q0, q0_end, (pack0, near0, far0), (n_last,))
    carried1 = early(1, q1, q1_end, (pack1, near1, far1), (pack0, near0, far0, n_last))
    end0, own0 = late(0, (1, 0), (q0_end, q0), last0, carried0)
    back0 = swap_side(end0)
    (end1,) = late(1, (1,), (q1_end,), last1, carried1)
    back1 = swap_side(end1)
    (own1,) = late(1, (0,), (q1,), last1, carried1)
    return call(join_body, sds(queries.shape), [VMEM] * 4, VMEM, nbytes=1 << 20)(
        own0, own1, back0, back1
    )


def passed_along(block, axis, distance):
    devices = range(lax.axis_size(axis))
    route = [(i - distance, i) for i in devices if i - distance in devices]
    return lax.ppermute(block, axis, route)


def passed_along_2(block, axis, distance):
    devices = range(lax.axis_size(axis))
    route = [((i - distance) % len(devices), i) for i in devices]
    return lax.ppermute(block, axis, route)


def ring_local(
    queries, new_keys, new_values, page_keys, page_values, page_table, page_slot, page_length
):
    query_rows = queries[0]
    rows_dev = query_rows.shape[0]
    key_width = new_keys.shape[2]
    shared_heads = key_width // HD
    query_count = query_rows.shape[1] // HD
    group_size = query_count // shared_heads
    scaling = 1.0 / math.sqrt(HD)
    position = lax.axis_index("ctx")
    cycle_size = lax.axis_size("ctx")
    pool_index = lax.axis_index("grp")
    request = position // SPAN
    row_ids = position * rows_dev + jnp.arange(rows_dev, dtype=jnp.int32)
    query_heads = query_rows.reshape(rows_dev, shared_heads, group_size, HD).transpose(1, 2, 0, 3)
    pages_total = page_slot.shape[1]
    numbers = jnp.arange(pages_total, dtype=jnp.int32)
    listed = jnp.any(page_table[0][:, :, None] == numbers[None, None, :], axis=1).astype(
        jnp.float32
    )
    own_listed = lax.dynamic_index_in_dim(listed, request, 0, keepdims=False)
    placed = (page_slot[0][:, None] == numbers[None, :]).astype(jnp.float32)
    listed_slot = jnp.dot(own_listed, placed, precision=lax.Precision.HIGHEST)
    length_slot = jnp.dot(
        page_length[0].astype(jnp.float32), placed, precision=lax.Precision.HIGHEST
    )
    offsets = jnp.arange(PAGE, dtype=jnp.int32).astype(jnp.float32)
    page_open = (listed_slot[:, None] > 0.5) & (offsets[None, :] < length_slot[:, None])
    page_limits = jnp.where(page_open, 0, far_limit).astype(jnp.int32).reshape(cycle_size, -1)

    def own_limits(holder):
        same = holder // SPAN == request
        return jnp.where(same, holder * rows_dev + jnp.arange(rows_dev, dtype=jnp.int32), far_limit)

    def taken_limits(holder):
        same = (holder // SPAN == request) & (pool_index == 1)
        return jnp.where(same, jnp.zeros((rows_dev,), jnp.int32), far_limit)

    def absorb_rows(carried, key_rows, value_rows, limits):
        maxima, totals, accumulated = carried
        pieces = key_rows.shape[0]
        key_heads = key_rows.reshape(pieces, shared_heads, HD)
        value_heads = value_rows.reshape(pieces, shared_heads, HD)
        scores = (
            jnp.einsum("kgrd,nkd->kgrn", query_heads, key_heads, preferred_element_type=jnp.float32)
            * scaling
        )
        allowed = row_ids[:, None] >= limits[None, :]
        masked = jnp.where(allowed, scores, neg_floor)
        new_max = jnp.maximum(maxima, jnp.max(masked, axis=-1))
        weights = jnp.where(allowed, jnp.exp(masked - new_max[..., None]), 0.0)
        rescale = jnp.exp(maxima - new_max)
        totals = totals * rescale + jnp.sum(weights, axis=-1)
        product = jnp.einsum(
            "kgrn,nkd->kgrd",
            weights.astype(jnp.bfloat16),
            value_heads,
            preferred_element_type=jnp.float32,
        )
        accumulated = accumulated * rescale[..., None] + product
        return (new_max, totals, accumulated)

    own_pairs = jnp.stack([new_keys[0], new_values[0]])
    taken_pairs = passed_along(own_pairs, "grp", 1)
    page_pairs = jnp.stack([page_keys[0], page_values[0]])
    carried = (
        jnp.full((shared_heads, group_size, rows_dev), neg_floor, jnp.float32),
        jnp.zeros((shared_heads, group_size, rows_dev), jnp.float32),
        jnp.zeros((shared_heads, group_size, rows_dev, HD), jnp.float32),
    )
    moving_rows = jnp.concatenate([page_pairs, own_pairs, taken_pairs], axis=1)

    def block_limits(holder):
        page_part = lax.dynamic_index_in_dim(page_limits, holder, 0, keepdims=False)
        return jnp.concatenate([page_part, own_limits(holder), taken_limits(holder)])

    def advance(stride, state_pair):
        inner, travelling = state_pair
        holder = (position - stride) % cycle_size
        inner = absorb_rows(inner, travelling[0], travelling[1], block_limits(holder))
        travelling = passed_along_2(travelling, "ctx", 1)
        return (inner, travelling)

    carried, moving_rows = lax.fori_loop(0, cycle_size - 1, advance, (carried, moving_rows))
    carried = absorb_rows(
        carried, moving_rows[0], moving_rows[1], block_limits((position + 1) % cycle_size)
    )
    _, totals, accumulated = carried
    attended = accumulated / totals[..., None]
    attended = attended.transpose(2, 0, 1, 3).reshape(rows_dev, query_count * HD)
    return attended.astype(jnp.bfloat16)[None]


def solution(mesh):
    in_specs = (
        P("grp", "ctx", "head"),
        P("grp", "ctx", "head"),
        P("grp", "ctx", "head"),
        P("grp", "ctx", "head"),
        P("grp", "ctx", "head"),
        P("grp", None, None),
        P("grp", None),
        P("grp", None),
    )
    chain = mesh.shape["ctx"] == SPAN == 4 and mesh.shape["grp"] == 2
    local = chain_local if chain else ring_local
    out_specs = P("grp", "ctx", "head")
    return jax.shard_map(local, mesh=mesh, in_specs=in_specs, out_specs=out_specs, check_vma=False)
```

```python
import functools
import math

import jax
import jax.numpy as jnp
from jax import lax
from jax.experimental import pallas as pl
from jax.experimental.pallas import tpu as pltpu
from jax.sharding import PartitionSpec as P


HD = 128
SPAN = 4
PAGE = 64
CAP = 6


neg_floor = -1e30
far_limit = 1 << 30
log2_scale = math.log2(math.e) / math.sqrt(HD)

HBM = pl.BlockSpec(memory_space=pltpu.HBM)
VMEM = pl.BlockSpec(memory_space=pltpu.VMEM)
SMEM = pl.BlockSpec(memory_space=pltpu.SMEM)


def call(body, outs, in_specs, out_specs, scratch=(), flops=0, nbytes=0):
    return pl.pallas_call(
        body,
        out_shape=outs,
        in_specs=in_specs,
        out_specs=out_specs,
        scratch_shapes=scratch,
        compiler_params=pltpu.CompilerParams(vmem_limit_bytes=40 << 20),
        cost_estimate=pl.CostEstimate(flops=flops, bytes_accessed=nbytes, transcendentals=0),
    )


def sds(shape, dtype=jnp.bfloat16):
    return jax.ShapeDtypeStruct(shape, dtype)


def listed_pages(tables, places, limits, source, count, most, sem):
    table, slot, length = places
    holders = lax.axis_size("ctx")
    held = slot.shape[1] // holders
    reads = [
        pltpu.make_async_copy(wide, near, sem.at[i])
        for i, (wide, near) in enumerate(zip(tables, places))
    ]
    for copy in reads:
        copy.start()
    for i in range(holders * held):
        limits[i] = 0
        source[i] = 0
    for i in range(holders):
        count[i] = 0
    for copy in reads:
        copy.wait()
    for i in range(table.shape[2]):
        number = table[0, 0, i]
        place = slot[0, number]
        holder = place // held
        nth = count[holder]
        count[holder] = nth + 1
        limits[holder * held + nth] = length[0, number]
        source[holder * held + nth] = place - holder * held
    for i in range(holders):
        limits[holders * held + i] = count[i]
    most[0] = functools.reduce(jnp.maximum, [count[i] for i in range(holders)])


def page_copies(packs, pages, source, first, cap, sem):
    position = lax.axis_index("ctx")
    held = source.shape[0] // lax.axis_size("ctx")
    copies = []
    for g, pack in enumerate(packs):
        for j in range(cap):
            row = pl.multiple_of(source[position * held + first + j] * PAGE, PAGE)
            for w, wide in enumerate(pages):
                copy = pltpu.make_async_copy(
                    wide.at[0, pl.ds(row, PAGE), pl.ds(g * HD, HD)],
                    pack.at[w, pl.ds(j * PAGE, PAGE), :],
                    sem.at[(j * 2 + g) * 2 + w],
                )
                copy.start()
                copies.append(copy)
    return copies


def pack_body(
    table_in, slot_in, length_in, pk, pv, nk, nv, q, pack0, pack1, fresh, q0, q1, limits, most,
    table, slot, length, source, count, sem, sem_new, *, cap
):
    half = q0.shape[1]
    rows_dev = nk.shape[1]
    copies = []
    for i, (wide, near) in enumerate(((0, q0), (half, q1))):
        copies.append(pltpu.make_async_copy(q.at[0, :, pl.ds(wide, half)], near, sem_new.at[i]))
    for w, new in enumerate((nk, nv)):
        for g in range(2):
            for n, (pack, row) in enumerate(((pack0, cap * PAGE), (fresh, 0))):
                copies.append(
                    pltpu.make_async_copy(
                        new.at[0, :, pl.ds(g * HD, HD)],
                        pack.at[w, pl.ds(row + g * rows_dev, rows_dev), :],
                        sem_new.at[2 + (n * 2 + w) * 2 + g],
                    )
                )
    for copy in copies:
        copy.start()
    listed_pages(
        (table_in, slot_in, length_in), (table, slot, length), limits, source, count, most, sem
    )
    copies += page_copies((pack0, pack1), (pk, pv), source, 0, cap, sem)
    for copy in copies:
        copy.wait()


def spare_body(
    table_in, slot_in, length_in, pk, pv, rest, table, slot, length, source, count, limits, most,
    sem, *, first, cap
):
    listed_pages(
        (table_in, slot_in, length_in), (table, slot, length), limits, source, count, most, sem
    )
    for copy in page_copies((rest.at[0], rest.at[1]), (pk, pv), source, first, cap, sem):
        copy.wait()


def blank_body(*refs):
    pass


def holder_ids(position):
    left = position < 2
    return (
        position,
        position ^ 1,
        jnp.where(left, 2, 1),
        jnp.where(left, 3, 0),
    )


def is_inner(position):
    return (position == 1) | (position == 2)


def heads_of(ref):
    return jnp.concatenate(
        [ref[:, i * HD : (i + 1) * HD] for i in range(ref.shape[1] // HD)], axis=0
    )


def page_bias(limits, first, count):
    column = lax.broadcasted_iota(jnp.int32, (1, count * PAGE), 1)
    page = column // PAGE
    within = column - page * PAGE
    limit = jnp.zeros((1, count * PAGE), jnp.int32)
    for j in range(count):
        limit = jnp.where(page == j, limits[first + j], limit)
    return jnp.where(within < limit, 0.0, neg_floor).astype(jnp.float32)


def held_pages(limits):
    holders = lax.axis_size("ctx")
    return limits.shape[0] // holders - 1


def join_limits(limits, ids, cap, joined):
    holders = lax.axis_size("ctx")
    held = held_pages(limits)
    for i in range(joined.shape[0]):
        joined[i] = 0
    offsets = []
    offset = jnp.int32(0)
    for holder in ids:
        offsets.append(offset)
        for j in range(cap):
            joined[offset + j] = limits[holder * held + j]
        offset = offset + jnp.minimum(limits[holders * held + holder], cap)
    return offsets, offset


def plan_body(limits, marks, bias_early, bias_late, bias_spare, joined, last, *, cap, early):
    holders = lax.axis_size("ctx")
    held = held_pages(limits)
    ids = holder_ids(lax.axis_index("ctx"))
    offsets, total = join_limits(limits, ids[:3], cap, joined)
    more = jnp.maximum(total - early, 0)
    for j in range(cap):
        last[j] = joined[early + j]
    for j in range(cap):
        last[more + j] = limits[ids[3] * held + j]
    most = functools.reduce(jnp.maximum, [limits[holders * held + i] for i in range(holders)])
    for i, mark in enumerate((offsets[1], offsets[2], more, most)):
        marks[i] = mark
    for ref, bias in (
        (bias_early, page_bias(joined, 0, early)),
        (bias_late, page_bias(last, 0, cap)),
    ):
        ref[...] = jnp.broadcast_to(bias, ref.shape)
    for i, holder in enumerate(ids):
        bias = page_bias(limits, holder * held + cap, held - cap)
        bias_spare[i] = jnp.broadcast_to(bias, bias_spare.shape[1:])


def place_pages(dense, packs, offsets, cap):
    for b, pack in enumerate(packs):
        dense[:, b * cap * PAGE : (b + 1) * cap * PAGE, :] = pack[:, : cap * PAGE, :]
    for pack, offset in list(zip(packs, offsets))[1:]:
        row = pl.multiple_of(offset * PAGE, PAGE)
        dense[:, pl.ds(row, cap * PAGE), :] = pack[:, : cap * PAGE, :]


def causal_bias(position, ids, rows, rows_dev):
    shape = (rows_dev, len(ids) * rows_dev)
    row = lax.broadcasted_iota(jnp.int32, shape, 0)
    column = lax.broadcasted_iota(jnp.int32, (1, shape[1]), 1)
    key = jnp.zeros_like(column)
    for i, holder in enumerate(ids):
        key = jnp.where(column // rows_dev == i, column + (holder - i) * rows_dev, key)
    allowed = position * rows_dev + row >= key
    bias = jnp.where(allowed, 0.0, neg_floor).astype(jnp.float32)
    return jnp.concatenate([bias] * (rows // rows_dev), axis=0)


def scored(q, k, bias):
    s = lax.dot_general(q, k, (((1,), (1,)), ((), ())), preferred_element_type=jnp.float32)
    return s * log2_scale + bias


def attend(q, blocks, state=None):
    scores = [scored(q, k, bias) for k, _, bias in blocks]
    shape = (q.shape[0], HD)
    top = functools.reduce(jnp.maximum, [jnp.max(s, axis=1, keepdims=True) for s in scores])
    if state is not None:
        old_top, old_total, old_acc = state
        wide = jnp.maximum(jnp.broadcast_to(top, shape), old_top)
        rescale = jnp.exp2(old_top - wide)
        top = wide[:, 0:1]
    total = 0.0
    acc = 0.0
    for s, (_, v, _) in zip(scores, blocks):
        w = jnp.exp2(s - top)
        total = total + jnp.sum(w, axis=1, keepdims=True)
        acc = acc + jnp.dot(w.astype(jnp.bfloat16), v, preferred_element_type=jnp.float32)
    if state is None:
        return top, total, acc
    total = jnp.broadcast_to(total, shape) + old_total * rescale
    return total, acc + old_acc * rescale


def early_body(marks, bias_early, q_own, q_end, *refs, cap, early, g):
    tops, totals, accs, left, dense = refs[-5:]
    packs = refs[:3]
    news = refs[3:7] if len(refs) == 12 else packs + refs[3:4]
    position = lax.axis_index("ctx")
    rows_dev = q_own.shape[0]
    rows = accs.shape[1]

    @pl.when(is_inner(position))
    def _():
        ids = holder_ids(position)
        place_pages(dense, packs, (0, marks[0], marks[1]), cap)
        firsts = [n.shape[1] - 2 * rows_dev + g * rows_dev for n in news]
        nk = jnp.concatenate([n[0, i : i + rows_dev] for n, i in zip(news, firsts)], axis=0)
        nv = jnp.concatenate([n[1, i : i + rows_dev] for n, i in zip(news, firsts)], axis=0)
        split = early * PAGE
        left[...] = dense[:, split : split + left.shape[1], :]
        paged = (dense[0, :split], dense[1, :split], bias_early[0:1, :])
        for t, q in enumerate((q_own, q_end)):
            fresh = (nk, nv, causal_bias(position ^ t, ids, rows, rows_dev))
            top, total, acc = attend(heads_of(q), [paged, fresh])
            tops[t] = jnp.broadcast_to(top, acc.shape)
            totals[t] = jnp.broadcast_to(total, acc.shape)
            accs[t] = acc


def late_body(*refs, cap, g, tasks):
    n = len(tasks)
    marks, bias_late, bias_spare = refs[:3]
    queries = refs[3 : 3 + n]
    pack, taken, left, tops, totals, accs = refs[3 + n : 9 + n]
    spilled = refs[9 + n : 13 + n]
    outs = refs[13 + n : 13 + 2 * n]
    extra, sem, dense = refs[13 + 2 * n :]

    def finish(more):
        rows_dev = queries[0].shape[0]
        place_pages(dense, (left, pack), (0, marks[2]), cap)
        new = slice(g * rows_dev, (g + 1) * rows_dev)
        shut = jnp.where(lax.axis_index("grp") == 1, 0.0, neg_floor).astype(jnp.float32)
        tk = jnp.concatenate([taken[i, 0, new] for i in range(taken.shape[0])], axis=0)
        tv = jnp.concatenate([taken[i, 1, new] for i in range(taken.shape[0])], axis=0)
        blocks = [
            (dense[0, : cap * PAGE], dense[1, : cap * PAGE], bias_late[0:1, :]),
            (tk, tv, jnp.full((1, tk.shape[0]), shut, jnp.float32)),
        ]
        if more:
            copies = [
                pltpu.make_async_copy(ref.at[g], extra.at[i], sem.at[i])
                for i, ref in enumerate(spilled)
            ]
            for copy in copies:
                copy.start()
            for copy in copies:
                copy.wait()
            for i in range(len(spilled)):
                blocks.append((extra[i, 0], extra[i, 1], bias_spare[i, 0:1, :]))
        for t, q, out in zip(tasks, queries, outs):
            total, num = attend(heads_of(q), blocks, (tops[t], totals[t], accs[t]))
            result = (num / total).astype(jnp.bfloat16)
            for i in range(out.shape[1] // HD):
                out[:, i * HD : (i + 1) * HD] = result[i * rows_dev : (i + 1) * rows_dev]

    inner = is_inner(lax.axis_index("ctx"))
    over = marks[3] > cap

    @pl.when(inner & jnp.logical_not(over))
    def _():
        finish(False)

    @pl.when(inner & over)
    def _():
        finish(True)


def join_body(own0, own1, back0, back1, out):
    inner = is_inner(lax.axis_index("ctx"))
    half = own0.shape[1]

    @pl.when(inner)
    def _():
        out[0, :, :half] = own0[...]
        out[0, :, half:] = own1[...]

    @pl.when(jnp.logical_not(inner))
    def _():
        out[0, :, :half] = back0[...]
        out[0, :, half:] = back1[...]


def chain_local(*args):
    return chain_steps(*args)


def chain_steps(
    queries, new_keys, new_values, page_keys, page_values, page_table, page_slot, page_length
):
    rows_dev = queries.shape[1]
    width = new_keys.shape[2]
    group = queries.shape[2] // width
    holders = lax.axis_size("ctx")
    heads = lax.axis_size("head")
    held = page_slot.shape[1] // holders
    cap = CAP
    keys = cap * PAGE
    side = [(i, i ^ 1) for i in range(holders)]
    middle = []
    for h in range(heads):
        other = h ^ 1 if h ^ 1 < heads else h
        for c in range(holders):
            if c in (1, 2):
                middle.append((c * heads + h, (3 - c) * heads + h))
            else:
                middle.append((c * heads + h, c * heads + other))

    def swap_side(x):
        return lax.ppermute(x, "ctx", side)

    def swap_middle(x):
        return lax.ppermute(x, ("ctx", "head"), middle)

    def swap_pools(x):
        return lax.ppermute(x, "grp", [(0, 1), (1, 0)])

    new_keys, new_values, queries, page_table, page_slot, page_length, page_keys, page_values = [
        pltpu.with_memory_space_constraint(x, pltpu.HBM)
        for x in (
            new_keys, new_values, queries, page_table, page_slot, page_length, page_keys,
            page_values,
        )
    ]
    half = sds((rows_dev, group * HD))
    tables = (page_table, page_slot, page_length, page_keys, page_values)
    scalars = [
        pltpu.SMEM(page_table.shape, jnp.int32),
        pltpu.SMEM(page_slot.shape, jnp.int32),
        pltpu.SMEM(page_length.shape, jnp.int32),
        pltpu.SMEM((holders * held,), jnp.int32),
        pltpu.SMEM((holders,), jnp.int32),
    ]
    pack0, pack1, fresh, q0, q1, limits, most = call(
        functools.partial(pack_body, cap=cap),
        (
            sds((2, keys + 2 * rows_dev, HD)),
            sds((2, keys, HD)),
            sds((2, 2 * rows_dev, HD)),
            half,
            half,
            sds((holders * held + holders,), jnp.int32),
            sds((1,), jnp.int32),
        ),
        [HBM] * 8,
        (VMEM,) * 5 + (SMEM, SMEM),
        scalars + [pltpu.SemaphoreType.DMA((cap * 4,)), pltpu.SemaphoreType.DMA((10,))],
        nbytes=3 << 20,
    )(*tables, new_keys, new_values, queries)

    near0 = swap_side(pack0)
    far0 = swap_middle(pack0)
    n_last = lax.ppermute(fresh, "ctx", [(0, 2), (2, 3), (3, 1), (1, 0)])
    q0_end = swap_side(q0)
    far1 = swap_middle(pack1)
    near1 = swap_side(pack1)
    last0 = swap_middle(near0[:, :keys])
    q1_end = swap_side(q1)
    taken = swap_pools(jnp.stack([fresh, near0[:, keys:], far0[:, keys:], n_last]))
    last1 = swap_middle(near1)
    early_pages = page_table.shape[2] - cap
    marks, bias_early, bias_late, bias_spare = call(
        functools.partial(plan_body, cap=cap, early=early_pages),
        (
            sds((8,), jnp.int32),
            sds((8, early_pages * PAGE), jnp.float32),
            sds((8, keys), jnp.float32),
            sds((holders, 8, (held - cap) * PAGE), jnp.float32),
        ),
        [SMEM],
        (SMEM, VMEM, VMEM, VMEM),
        [pltpu.SMEM((early_pages + 2 * cap,), jnp.int32), pltpu.SMEM((2 * cap,), jnp.int32)],
        nbytes=1 << 19,
    )(limits)
    spare = sds((2, 2, (held - cap) * PAGE, HD))

    def fetch():
        rest = call(
            functools.partial(spare_body, first=cap, cap=held - cap),
            spare,
            [HBM] * 5,
            VMEM,
            scalars
            + [
                pltpu.SMEM((holders * held + holders,), jnp.int32),
                pltpu.SMEM((1,), jnp.int32),
                pltpu.SemaphoreType.DMA((max(held - cap, 1) * 4,)),
            ],
            nbytes=1 << 20,
        )(*tables)
        near = swap_side(rest)
        far = swap_middle(rest)
        return rest, near, far, swap_middle(near)

    def skip():
        return tuple(call(blank_body, (spare,) * 4, [], (HBM,) * 4)())

    spilled = lax.cond(most[0] > cap, fetch, skip)

    rows = group * rows_dev
    pair_flops = 4 * rows * HD
    state = (sds((2, rows, HD), jnp.float32),) * 3 + (sds((2, keys, HD)),)

    def early(g, q, q_end, packs, news):
        return call(
            functools.partial(early_body, cap=cap, early=early_pages, g=g),
            state,
            [SMEM] + [VMEM] * (6 + len(news)),
            (VMEM,) * 4,
            [pltpu.VMEM((2, (early_pages + 2 * cap) * PAGE, HD), jnp.bfloat16)],
            flops=2 * pair_flops * (early_pages * PAGE + 4 * rows_dev),
            nbytes=4 << 20,
        )(marks, bias_early, q, q_end, *packs, *news)

    def late(g, tasks, queries, pack, carried):
        tops, totals, accs, left = carried
        return call(
            functools.partial(late_body, cap=cap, g=g, tasks=tasks),
            (half,) * len(tasks),
            [SMEM] + [VMEM] * (8 + len(tasks)) + [HBM] * 4,
            (VMEM,) * len(tasks),
            [
                pltpu.VMEM((4, 2, (held - cap) * PAGE, HD), jnp.bfloat16),
                pltpu.SemaphoreType.DMA((4,)),
                pltpu.VMEM((2, 2 * keys, HD), jnp.bfloat16),
            ],
            flops=len(tasks) * pair_flops * (keys + 4 * rows_dev),
            nbytes=len(tasks) << 20,
        )(marks, bias_late, bias_spare, *queries, pack, taken, left, tops, totals, accs, *spilled)

    carried0 = early(0, q0, q0_end, (pack0, near0, far0), (n_last,))
    carried1 = early(1, q1, q1_end, (pack1, near1, far1), (pack0, near0, far0, n_last))
    end0, own0 = late(0, (1, 0), (q0_end, q0), last0, carried0)
    back0 = swap_side(end0)
    (end1,) = late(1, (1,), (q1_end,), last1, carried1)
    back1 = swap_side(end1)
    (own1,) = late(1, (0,), (q1,), last1, carried1)
    return call(join_body, sds(queries.shape), [VMEM] * 4, VMEM, nbytes=1 << 20)(
        own0, own1, back0, back1
    )


def passed_along(block, axis, distance):
    devices = range(lax.axis_size(axis))
    route = [(i - distance, i) for i in devices if i - distance in devices]
    return lax.ppermute(block, axis, route)


def passed_along_2(block, axis, distance):
    devices = range(lax.axis_size(axis))
    route = [((i - distance) % len(devices), i) for i in devices]
    return lax.ppermute(block, axis, route)


def ring_local(
    queries, new_keys, new_values, page_keys, page_values, page_table, page_slot, page_length
):
    query_rows = queries[0]
    rows_dev = query_rows.shape[0]
    key_width = new_keys.shape[2]
    shared_heads = key_width // HD
    query_count = query_rows.shape[1] // HD
    group_size = query_count // shared_heads
    scaling = 1.0 / math.sqrt(HD)
    position = lax.axis_index("ctx")
    cycle_size = lax.axis_size("ctx")
    pool_index = lax.axis_index("grp")
    request = position // SPAN
    row_ids = position * rows_dev + jnp.arange(rows_dev, dtype=jnp.int32)
    query_heads = query_rows.reshape(rows_dev, shared_heads, group_size, HD).transpose(1, 2, 0, 3)
    pages_total = page_slot.shape[1]
    numbers = jnp.arange(pages_total, dtype=jnp.int32)
    listed = jnp.any(page_table[0][:, :, None] == numbers[None, None, :], axis=1).astype(
        jnp.float32
    )
    own_listed = lax.dynamic_index_in_dim(listed, request, 0, keepdims=False)
    placed = (page_slot[0][:, None] == numbers[None, :]).astype(jnp.float32)
    listed_slot = jnp.dot(own_listed, placed, precision=lax.Precision.HIGHEST)
    length_slot = jnp.dot(
        page_length[0].astype(jnp.float32), placed, precision=lax.Precision.HIGHEST
    )
    offsets = jnp.arange(PAGE, dtype=jnp.int32).astype(jnp.float32)
    page_open = (listed_slot[:, None] > 0.5) & (offsets[None, :] < length_slot[:, None])
    page_limits = jnp.where(page_open, 0, far_limit).astype(jnp.int32).reshape(cycle_size, -1)

    def own_limits(holder):
        same = holder // SPAN == request
        return jnp.where(same, holder * rows_dev + jnp.arange(rows_dev, dtype=jnp.int32), far_limit)

    def taken_limits(holder):
        same = (holder // SPAN == request) & (pool_index == 1)
        return jnp.where(same, jnp.zeros((rows_dev,), jnp.int32), far_limit)

    def absorb_rows(carried, key_rows, value_rows, limits):
        maxima, totals, accumulated = carried
        pieces = key_rows.shape[0]
        key_heads = key_rows.reshape(pieces, shared_heads, HD)
        value_heads = value_rows.reshape(pieces, shared_heads, HD)
        scores = (
            jnp.einsum("kgrd,nkd->kgrn", query_heads, key_heads, preferred_element_type=jnp.float32)
            * scaling
        )
        allowed = row_ids[:, None] >= limits[None, :]
        masked = jnp.where(allowed, scores, neg_floor)
        new_max = jnp.maximum(maxima, jnp.max(masked, axis=-1))
        weights = jnp.where(allowed, jnp.exp(masked - new_max[..., None]), 0.0)
        rescale = jnp.exp(maxima - new_max)
        totals = totals * rescale + jnp.sum(weights, axis=-1)
        product = jnp.einsum(
            "kgrn,nkd->kgrd",
            weights.astype(jnp.bfloat16),
            value_heads,
            preferred_element_type=jnp.float32,
        )
        accumulated = accumulated * rescale[..., None] + product
        return (new_max, totals, accumulated)

    own_pairs = jnp.stack([new_keys[0], new_values[0]])
    taken_pairs = passed_along(own_pairs, "grp", 1)
    page_pairs = jnp.stack([page_keys[0], page_values[0]])
    carried = (
        jnp.full((shared_heads, group_size, rows_dev), neg_floor, jnp.float32),
        jnp.zeros((shared_heads, group_size, rows_dev), jnp.float32),
        jnp.zeros((shared_heads, group_size, rows_dev, HD), jnp.float32),
    )
    moving_rows = jnp.concatenate([page_pairs, own_pairs, taken_pairs], axis=1)

    def block_limits(holder):
        page_part = lax.dynamic_index_in_dim(page_limits, holder, 0, keepdims=False)
        return jnp.concatenate([page_part, own_limits(holder), taken_limits(holder)])

    def advance(stride, state_pair):
        inner, travelling = state_pair
        holder = (position - stride) % cycle_size
        inner = absorb_rows(inner, travelling[0], travelling[1], block_limits(holder))
        travelling = passed_along_2(travelling, "ctx", 1)
        return (inner, travelling)

    carried, moving_rows = lax.fori_loop(0, cycle_size - 1, advance, (carried, moving_rows))
    carried = absorb_rows(
        carried, moving_rows[0], moving_rows[1], block_limits((position + 1) % cycle_size)
    )
    _, totals, accumulated = carried
    attended = accumulated / totals[..., None]
    attended = attended.transpose(2, 0, 1, 3).reshape(rows_dev, query_count * HD)
    return attended.astype(jnp.bfloat16)[None]


def solution(mesh):
    in_specs = (
        P("grp", "ctx", "head"),
        P("grp", "ctx", "head"),
        P("grp", "ctx", "head"),
        P("grp", "ctx", "head"),
        P("grp", "ctx", "head"),
        P("grp", None, None),
        P("grp", None),
        P("grp", None),
    )
    chain = mesh.shape["ctx"] == SPAN == 4 and mesh.shape["grp"] == 2
    local = chain_local if chain else ring_local
    out_specs = P("grp", "ctx", "head")
    return jax.shard_map(local, mesh=mesh, in_specs=in_specs, out_specs=out_specs, check_vma=False)
```

```python
import functools
import math

import jax
import jax.numpy as jnp
from jax import lax
from jax.experimental import pallas as pl
from jax.experimental.pallas import tpu as pltpu
from jax.sharding import PartitionSpec as P


HD = 128
SPAN = 4
PAGE = 64
CAP = 6


neg_floor = -1e30
far_limit = 1 << 30
log2_scale = math.log2(math.e) / math.sqrt(HD)

HBM = pl.BlockSpec(memory_space=pltpu.HBM)
VMEM = pl.BlockSpec(memory_space=pltpu.VMEM)
SMEM = pl.BlockSpec(memory_space=pltpu.SMEM)


def call(body, outs, in_specs, out_specs, scratch=(), flops=0, nbytes=0):
    return pl.pallas_call(
        body,
        out_shape=outs,
        in_specs=in_specs,
        out_specs=out_specs,
        scratch_shapes=scratch,
        compiler_params=pltpu.CompilerParams(vmem_limit_bytes=40 << 20),
        cost_estimate=pl.CostEstimate(flops=flops, bytes_accessed=nbytes, transcendentals=0),
    )


def sds(shape, dtype=jnp.bfloat16):
    return jax.ShapeDtypeStruct(shape, dtype)


def listed_pages(tables, places, limits, source, count, most, sem):
    table, slot, length = places
    holders = lax.axis_size("ctx")
    held = slot.shape[1] // holders
    reads = [
        pltpu.make_async_copy(wide, near, sem.at[i])
        for i, (wide, near) in enumerate(zip(tables, places))
    ]
    for copy in reads:
        copy.start()
    for i in range(holders * held):
        limits[i] = 0
        source[i] = 0
    for i in range(holders):
        count[i] = 0
    for copy in reads:
        copy.wait()
    for i in range(table.shape[2]):
        number = table[0, 0, i]
        place = slot[0, number]
        holder = place // held
        nth = count[holder]
        count[holder] = nth + 1
        limits[holder * held + nth] = length[0, number]
        source[holder * held + nth] = place - holder * held
    for i in range(holders):
        limits[holders * held + i] = count[i]
    most[0] = functools.reduce(jnp.maximum, [count[i] for i in range(holders)])


def page_copies(packs, pages, source, first, cap, sem):
    position = lax.axis_index("ctx")
    held = source.shape[0] // lax.axis_size("ctx")
    copies = []
    for g, pack in enumerate(packs):
        for j in range(cap):
            row = pl.multiple_of(source[position * held + first + j] * PAGE, PAGE)
            for w, wide in enumerate(pages):
                copy = pltpu.make_async_copy(
                    wide.at[0, pl.ds(row, PAGE), pl.ds(g * HD, HD)],
                    pack.at[w, pl.ds(j * PAGE, PAGE), :],
                    sem.at[(j * 2 + g) * 2 + w],
                )
                copy.start()
                copies.append(copy)
    return copies


def pack_body(
    table_in, slot_in, length_in, pk, pv, nk, nv, pack0, pack1, fresh, limits, most,
    table, slot, length, source, count, sem, sem_new, *, cap
):
    rows_dev = nk.shape[1]
    copies = []
    for w, new in enumerate((nk, nv)):
        for g in range(2):
            for n, (pack, row) in enumerate(((pack0, cap * PAGE), (fresh, 0))):
                copies.append(
                    pltpu.make_async_copy(
                        new.at[0, :, pl.ds(g * HD, HD)],
                        pack.at[w, pl.ds(row + g * rows_dev, rows_dev), :],
                        sem_new.at[(n * 2 + w) * 2 + g],
                    )
                )
    for copy in copies:
        copy.start()
    listed_pages(
        (table_in, slot_in, length_in), (table, slot, length), limits, source, count, most, sem
    )
    copies += page_copies((pack0, pack1), (pk, pv), source, 0, cap, sem)
    for copy in copies:
        copy.wait()


def spare_body(
    table_in, slot_in, length_in, pk, pv, rest, table, slot, length, source, count, limits, most,
    sem, *, first, cap
):
    listed_pages(
        (table_in, slot_in, length_in), (table, slot, length), limits, source, count, most, sem
    )
    for copy in page_copies((rest.at[0], rest.at[1]), (pk, pv), source, first, cap, sem):
        copy.wait()


def blank_body(*refs):
    pass


def holder_ids(position):
    left = position < 2
    return (
        position,
        position ^ 1,
        jnp.where(left, 2, 1),
        jnp.where(left, 3, 0),
    )


def is_inner(position):
    return (position == 1) | (position == 2)


def heads_of(ref, g):
    group = ref.shape[2] // HD // 2
    return jnp.concatenate(
        [ref[0, :, i * HD : (i + 1) * HD] for i in range(g * group, (g + 1) * group)], axis=0
    )


def page_bias(limits, first, count):
    column = lax.broadcasted_iota(jnp.int32, (1, count * PAGE), 1)
    page = column // PAGE
    within = column - page * PAGE
    limit = jnp.zeros((1, count * PAGE), jnp.int32)
    for j in range(count):
        limit = jnp.where(page == j, limits[first + j], limit)
    return jnp.where(within < limit, 0.0, neg_floor).astype(jnp.float32)


def held_pages(limits):
    holders = lax.axis_size("ctx")
    return limits.shape[0] // holders - 1


def join_limits(limits, ids, cap, joined):
    holders = lax.axis_size("ctx")
    held = held_pages(limits)
    for i in range(joined.shape[0]):
        joined[i] = 0
    offsets = []
    offset = jnp.int32(0)
    for holder in ids:
        offsets.append(offset)
        for j in range(cap):
            joined[offset + j] = limits[holder * held + j]
        offset = offset + jnp.minimum(limits[holders * held + holder], cap)
    return offsets, offset


def plan_body(limits, marks, bias_early, bias_late, bias_spare, joined, last, *, cap, early):
    holders = lax.axis_size("ctx")
    held = held_pages(limits)
    ids = holder_ids(lax.axis_index("ctx"))
    offsets, total = join_limits(limits, ids[:3], cap, joined)
    more = jnp.maximum(total - early, 0)
    for j in range(cap):
        last[j] = joined[early + j]
    for j in range(cap):
        last[more + j] = limits[ids[3] * held + j]
    most = functools.reduce(jnp.maximum, [limits[holders * held + i] for i in range(holders)])
    for i, mark in enumerate((offsets[1], offsets[2], more, most)):
        marks[i] = mark
    for ref, bias in (
        (bias_early, page_bias(joined, 0, early)),
        (bias_late, page_bias(last, 0, cap)),
    ):
        ref[...] = jnp.broadcast_to(bias, ref.shape)
    for i, holder in enumerate(ids):
        bias = page_bias(limits, holder * held + cap, held - cap)
        bias_spare[i] = jnp.broadcast_to(bias, bias_spare.shape[1:])


def place_pages(dense, packs, offsets, cap):
    for b, pack in enumerate(packs):
        dense[:, b * cap * PAGE : (b + 1) * cap * PAGE, :] = pack[:, : cap * PAGE, :]
    for pack, offset in list(zip(packs, offsets))[1:]:
        row = pl.multiple_of(offset * PAGE, PAGE)
        dense[:, pl.ds(row, cap * PAGE), :] = pack[:, : cap * PAGE, :]


def causal_bias(position, ids, rows, rows_dev):
    shape = (rows_dev, len(ids) * rows_dev)
    row = lax.broadcasted_iota(jnp.int32, shape, 0)
    column = lax.broadcasted_iota(jnp.int32, (1, shape[1]), 1)
    key = jnp.zeros_like(column)
    for i, holder in enumerate(ids):
        key = jnp.where(column // rows_dev == i, column + (holder - i) * rows_dev, key)
    allowed = position * rows_dev + row >= key
    bias = jnp.where(allowed, 0.0, neg_floor).astype(jnp.float32)
    return jnp.concatenate([bias] * (rows // rows_dev), axis=0)


def scores_of(q, blocks):
    return [
        lax.dot_general(q, k, (((1,), (1,)), ((), ())), preferred_element_type=jnp.float32)
        for k, _, _ in blocks
    ]


def softmax_of(raw, blocks, state=None):
    scores = [s * log2_scale + bias for s, (_, _, bias) in zip(raw, blocks)]
    shape = (raw[0].shape[0], HD)
    top = functools.reduce(jnp.maximum, [jnp.max(s, axis=1, keepdims=True) for s in scores])
    if state is not None:
        old_top, old_total, old_acc = state
        wide = jnp.maximum(jnp.broadcast_to(top, shape), old_top)
        rescale = jnp.exp2(old_top - wide)
        top = wide[:, 0:1]
    total = 0.0
    acc = 0.0
    for s, (_, v, _) in zip(scores, blocks):
        w = jnp.exp2(s - top)
        total = total + jnp.sum(w, axis=1, keepdims=True)
        acc = acc + jnp.dot(w.astype(jnp.bfloat16), v, preferred_element_type=jnp.float32)
    if state is None:
        return top, total, acc
    total = jnp.broadcast_to(total, shape) + old_total * rescale
    return total, acc + old_acc * rescale


def in_turn(units):
    pending = None
    for queries, blocks, use in units:
        raw = scores_of(queries(), blocks)
        if pending is not None:
            pending()
        pending = functools.partial(use, raw, blocks)
    pending()


def early_body(marks, bias_early, q, *refs, cap, early, gs, t):
    news = refs[:4]
    packs = {0: news[:3], 1: refs[4:7] if 1 in gs else None}
    refs = refs[7 if 1 in gs else 4 :]
    tops, totals, accs = refs[:3]
    left = refs[3] if t else None
    dense = refs[-1]
    position = lax.axis_index("ctx")
    rows_dev = q.shape[1]
    rows = accs.shape[1]
    split = early * PAGE

    def blocks_of(u, g):
        ids = holder_ids(position)
        place_pages(dense.at[u], packs[g], (0, marks[0], marks[1]), cap)
        firsts = [n.shape[1] - 2 * rows_dev + g * rows_dev for n in news]
        nk = jnp.concatenate([n[0, i : i + rows_dev] for n, i in zip(news, firsts)], axis=0)
        nv = jnp.concatenate([n[1, i : i + rows_dev] for n, i in zip(news, firsts)], axis=0)
        if left is not None:
            left[...] = dense[u, :, split : split + left.shape[1], :]
        paged = (dense[u, 0, :split], dense[u, 1, :split], bias_early[0:1, :])
        return [paged, (nk, nv, causal_bias(position ^ t, ids, rows, rows_dev))]

    def keep(u, raw, blocks):
        top, total, acc = softmax_of(raw, blocks)
        tops[u] = jnp.broadcast_to(top, acc.shape)
        totals[u] = jnp.broadcast_to(total, acc.shape)
        accs[u] = acc

    @pl.when(is_inner(position))
    def _():
        in_turn(
            (functools.partial(heads_of, q, g), blocks_of(u, g), functools.partial(keep, u))
            for u, g in enumerate(gs)
        )


def late_body(marks, bias_late, bias_spare, q, taken, tops, totals, accs, *refs, cap, gs):
    n = len(gs)
    lasts, lefts, spilled, outs = (refs[a:b] for a, b in ((0, n), (n, 2 * n), (2 * n, 2 * n + 4), (2 * n + 4, 3 * n + 4)))
    extra, sem, dense = refs[3 * n + 4 :]
    rows_dev = q.shape[1]

    def blocks_of(u, g, more):
        place_pages(dense.at[u], (lefts[u], lasts[u]), (0, marks[2]), cap)
        new = slice(g * rows_dev, (g + 1) * rows_dev)
        shut = jnp.where(lax.axis_index("grp") == 1, 0.0, neg_floor).astype(jnp.float32)
        tk = jnp.concatenate([taken[i, 0, new] for i in range(taken.shape[0])], axis=0)
        tv = jnp.concatenate([taken[i, 1, new] for i in range(taken.shape[0])], axis=0)
        blocks = [
            (dense[u, 0, : cap * PAGE], dense[u, 1, : cap * PAGE], bias_late[0:1, :]),
            (tk, tv, jnp.full((1, tk.shape[0]), shut, jnp.float32)),
        ]
        if more:
            copies = [
                pltpu.make_async_copy(ref.at[g], extra.at[u, i], sem.at[i])
                for i, ref in enumerate(spilled)
            ]
            for copy in copies:
                copy.start()
            for copy in copies:
                copy.wait()
            for i in range(len(spilled)):
                blocks.append((extra[u, i, 0], extra[u, i, 1], bias_spare[i, 0:1, :]))
        return blocks

    def finish(more):
        for u, g in enumerate(gs):
            blocks = blocks_of(u, g, more)
            raw = scores_of(heads_of(q, g), blocks)
            total, num = softmax_of(raw, blocks, (tops[u], totals[u], accs[u]))
            result = (num / total).astype(jnp.bfloat16)
            for i in range(outs[u].shape[1] // HD):
                outs[u][:, i * HD : (i + 1) * HD] = result[i * rows_dev : (i + 1) * rows_dev]

    inner = is_inner(lax.axis_index("ctx"))
    over = marks[3] > cap

    @pl.when(inner & jnp.logical_not(over))
    def _():
        finish(False)

    @pl.when(inner & over)
    def _():
        finish(True)


def join_body(own0, own1, back0, back1, out):
    inner = is_inner(lax.axis_index("ctx"))
    half = own0.shape[1]

    @pl.when(inner)
    def _():
        out[0, :, :half] = own0[...]
        out[0, :, half:] = own1[...]

    @pl.when(jnp.logical_not(inner))
    def _():
        out[0, :, :half] = back0[...]
        out[0, :, half:] = back1[...]


def chain_local(*args):
    return chain_steps(*args)


def chain_steps(
    queries, new_keys, new_values, page_keys, page_values, page_table, page_slot, page_length
):
    rows_dev = queries.shape[1]
    width = new_keys.shape[2]
    group = queries.shape[2] // width
    holders = lax.axis_size("ctx")
    heads = lax.axis_size("head")
    held = page_slot.shape[1] // holders
    cap = CAP
    keys = cap * PAGE
    side = [(i, i ^ 1) for i in range(holders)]
    middle = []
    for h in range(heads):
        other = h ^ 1 if h ^ 1 < heads else h
        for c in range(holders):
            if c in (1, 2):
                middle.append((c * heads + h, (3 - c) * heads + h))
            else:
                middle.append((c * heads + h, c * heads + other))

    def swap_side(x):
        return lax.ppermute(x, "ctx", side)

    def swap_middle(x):
        return lax.ppermute(x, ("ctx", "head"), middle)

    def swap_pools(x):
        return lax.ppermute(x, "grp", [(0, 1), (1, 0)])

    new_keys, new_values, page_table, page_slot, page_length, page_keys, page_values = [
        pltpu.with_memory_space_constraint(x, pltpu.HBM)
        for x in (
            new_keys, new_values, page_table, page_slot, page_length, page_keys, page_values,
        )
    ]
    half = sds((rows_dev, group * HD))
    q_end = swap_side(queries)
    tables = (page_table, page_slot, page_length, page_keys, page_values)
    scalars = [
        pltpu.SMEM(page_table.shape, jnp.int32),
        pltpu.SMEM(page_slot.shape, jnp.int32),
        pltpu.SMEM(page_length.shape, jnp.int32),
        pltpu.SMEM((holders * held,), jnp.int32),
        pltpu.SMEM((holders,), jnp.int32),
    ]
    pack0, pack1, fresh, limits, most = call(
        functools.partial(pack_body, cap=cap),
        (
            sds((2, keys + 2 * rows_dev, HD)),
            sds((2, keys, HD)),
            sds((2, 2 * rows_dev, HD)),
            sds((holders * held + holders,), jnp.int32),
            sds((1,), jnp.int32),
        ),
        [HBM] * 7,
        (VMEM,) * 3 + (SMEM, SMEM),
        scalars + [pltpu.SemaphoreType.DMA((cap * 4,)), pltpu.SemaphoreType.DMA((8,))],
        nbytes=3 << 20,
    )(*tables, new_keys, new_values)

    near0 = swap_side(pack0)
    far0 = swap_middle(pack0)
    n_last = lax.ppermute(fresh, "ctx", [(0, 2), (2, 3), (3, 1), (1, 0)])
    far1 = swap_middle(pack1)
    near1 = swap_side(pack1)
    last0 = swap_middle(near0[:, :keys])
    taken = swap_pools(jnp.stack([fresh, near0[:, keys:], far0[:, keys:], n_last]))
    last1 = swap_middle(near1)
    early_pages = page_table.shape[2] - cap
    marks, bias_early, bias_late, bias_spare = call(
        functools.partial(plan_body, cap=cap, early=early_pages),
        (
            sds((8,), jnp.int32),
            sds((8, early_pages * PAGE), jnp.float32),
            sds((8, keys), jnp.float32),
            sds((holders, 8, (held - cap) * PAGE), jnp.float32),
        ),
        [SMEM],
        (SMEM, VMEM, VMEM, VMEM),
        [pltpu.SMEM((early_pages + 2 * cap,), jnp.int32), pltpu.SMEM((2 * cap,), jnp.int32)],
        nbytes=1 << 19,
    )(limits)
    spare = sds((2, 2, (held - cap) * PAGE, HD))

    def fetch():
        rest = call(
            functools.partial(spare_body, first=cap, cap=held - cap),
            spare,
            [HBM] * 5,
            VMEM,
            scalars
            + [
                pltpu.SMEM((holders * held + holders,), jnp.int32),
                pltpu.SMEM((1,), jnp.int32),
                pltpu.SemaphoreType.DMA((max(held - cap, 1) * 4,)),
            ],
            nbytes=1 << 20,
        )(*tables)
        near = swap_side(rest)
        far = swap_middle(rest)
        return rest, near, far, swap_middle(near)

    def skip():
        return tuple(call(blank_body, (spare,) * 4, [], (HBM,) * 4)())

    spilled = lax.cond(most[0] > cap, fetch, skip)

    rows = group * rows_dev
    pair_flops = 4 * rows * HD
    news = (pack0, near0, far0, n_last)

    def early(gs, q, t):
        n = len(gs)
        packs = (pack1, near1, far1) if 1 in gs else ()
        outs = (sds((n, rows, HD), jnp.float32),) * 3 + ((sds((2, keys, HD)),) if t else ())
        return call(
            functools.partial(early_body, cap=cap, early=early_pages, gs=gs, t=t),
            outs,
            [SMEM] + [VMEM] * (6 + len(packs)),
            (VMEM,) * len(outs),
            [pltpu.VMEM((n, 2, (early_pages + 2 * cap) * PAGE, HD), jnp.bfloat16)],
            flops=n * pair_flops * (early_pages * PAGE + 4 * rows_dev),
            nbytes=2 << 20,
        )(marks, bias_early, q, *news, *packs)

    def late(gs, q, carried, lefts):
        n = len(gs)
        return call(
            functools.partial(late_body, cap=cap, gs=gs),
            (half,) * n,
            [SMEM] + [VMEM] * (7 + 2 * n) + [HBM] * 4,
            (VMEM,) * n,
            [
                pltpu.VMEM((n, 4, 2, (held - cap) * PAGE, HD), jnp.bfloat16),
                pltpu.SemaphoreType.DMA((4,)),
                pltpu.VMEM((n, 2, 2 * keys, HD), jnp.bfloat16),
            ],
            flops=n * pair_flops * (keys + 4 * rows_dev),
            nbytes=n << 20,
        )(
            marks, bias_late, bias_spare, q, taken, *carried, *[(last0, last1)[g] for g in gs],
            *lefts, *spilled,
        )

    *end_state0, left0 = early((0,), q_end, 1)
    *end_state1, left1 = early((1,), q_end, 1)
    own_state = early((0, 1), queries, 0)
    (end0,) = late((0,), q_end, end_state0, (left0,))
    back0 = swap_side(end0)
    (end1,) = late((1,), q_end, end_state1, (left1,))
    back1 = swap_side(end1)
    own0, own1 = late((0, 1), queries, own_state, (left0, left1))
    return call(join_body, sds(queries.shape), [VMEM] * 4, VMEM, nbytes=1 << 20)(
        own0, own1, back0, back1
    )


def passed_along(block, axis, distance):
    devices = range(lax.axis_size(axis))
    route = [(i - distance, i) for i in devices if i - distance in devices]
    return lax.ppermute(block, axis, route)


def passed_along_2(block, axis, distance):
    devices = range(lax.axis_size(axis))
    route = [((i - distance) % len(devices), i) for i in devices]
    return lax.ppermute(block, axis, route)


def ring_local(
    queries, new_keys, new_values, page_keys, page_values, page_table, page_slot, page_length
):
    query_rows = queries[0]
    rows_dev = query_rows.shape[0]
    key_width = new_keys.shape[2]
    shared_heads = key_width // HD
    query_count = query_rows.shape[1] // HD
    group_size = query_count // shared_heads
    scaling = 1.0 / math.sqrt(HD)
    position = lax.axis_index("ctx")
    cycle_size = lax.axis_size("ctx")
    pool_index = lax.axis_index("grp")
    request = position // SPAN
    row_ids = position * rows_dev + jnp.arange(rows_dev, dtype=jnp.int32)
    query_heads = query_rows.reshape(rows_dev, shared_heads, group_size, HD).transpose(1, 2, 0, 3)
    pages_total = page_slot.shape[1]
    numbers = jnp.arange(pages_total, dtype=jnp.int32)
    listed = jnp.any(page_table[0][:, :, None] == numbers[None, None, :], axis=1).astype(
        jnp.float32
    )
    own_listed = lax.dynamic_index_in_dim(listed, request, 0, keepdims=False)
    placed = (page_slot[0][:, None] == numbers[None, :]).astype(jnp.float32)
    listed_slot = jnp.dot(own_listed, placed, precision=lax.Precision.HIGHEST)
    length_slot = jnp.dot(
        page_length[0].astype(jnp.float32), placed, precision=lax.Precision.HIGHEST
    )
    offsets = jnp.arange(PAGE, dtype=jnp.int32).astype(jnp.float32)
    page_open = (listed_slot[:, None] > 0.5) & (offsets[None, :] < length_slot[:, None])
    page_limits = jnp.where(page_open, 0, far_limit).astype(jnp.int32).reshape(cycle_size, -1)

    def own_limits(holder):
        same = holder // SPAN == request
        return jnp.where(same, holder * rows_dev + jnp.arange(rows_dev, dtype=jnp.int32), far_limit)

    def taken_limits(holder):
        same = (holder // SPAN == request) & (pool_index == 1)
        return jnp.where(same, jnp.zeros((rows_dev,), jnp.int32), far_limit)

    def absorb_rows(carried, key_rows, value_rows, limits):
        maxima, totals, accumulated = carried
        pieces = key_rows.shape[0]
        key_heads = key_rows.reshape(pieces, shared_heads, HD)
        value_heads = value_rows.reshape(pieces, shared_heads, HD)
        scores = (
            jnp.einsum("kgrd,nkd->kgrn", query_heads, key_heads, preferred_element_type=jnp.float32)
            * scaling
        )
        allowed = row_ids[:, None] >= limits[None, :]
        masked = jnp.where(allowed, scores, neg_floor)
        new_max = jnp.maximum(maxima, jnp.max(masked, axis=-1))
        weights = jnp.where(allowed, jnp.exp(masked - new_max[..., None]), 0.0)
        rescale = jnp.exp(maxima - new_max)
        totals = totals * rescale + jnp.sum(weights, axis=-1)
        product = jnp.einsum(
            "kgrn,nkd->kgrd",
            weights.astype(jnp.bfloat16),
            value_heads,
            preferred_element_type=jnp.float32,
        )
        accumulated = accumulated * rescale[..., None] + product
        return (new_max, totals, accumulated)

    own_pairs = jnp.stack([new_keys[0], new_values[0]])
    taken_pairs = passed_along(own_pairs, "grp", 1)
    page_pairs = jnp.stack([page_keys[0], page_values[0]])
    carried = (
        jnp.full((shared_heads, group_size, rows_dev), neg_floor, jnp.float32),
        jnp.zeros((shared_heads, group_size, rows_dev), jnp.float32),
        jnp.zeros((shared_heads, group_size, rows_dev, HD), jnp.float32),
    )
    moving_rows = jnp.concatenate([page_pairs, own_pairs, taken_pairs], axis=1)

    def block_limits(holder):
        page_part = lax.dynamic_index_in_dim(page_limits, holder, 0, keepdims=False)
        return jnp.concatenate([page_part, own_limits(holder), taken_limits(holder)])

    def advance(stride, state_pair):
        inner, travelling = state_pair
        holder = (position - stride) % cycle_size
        inner = absorb_rows(inner, travelling[0], travelling[1], block_limits(holder))
        travelling = passed_along_2(travelling, "ctx", 1)
        return (inner, travelling)

    carried, moving_rows = lax.fori_loop(0, cycle_size - 1, advance, (carried, moving_rows))
    carried = absorb_rows(
        carried, moving_rows[0], moving_rows[1], block_limits((position + 1) % cycle_size)
    )
    _, totals, accumulated = carried
    attended = accumulated / totals[..., None]
    attended = attended.transpose(2, 0, 1, 3).reshape(rows_dev, query_count * HD)
    return attended.astype(jnp.bfloat16)[None]


def solution(mesh):
    in_specs = (
        P("grp", "ctx", "head"),
        P("grp", "ctx", "head"),
        P("grp", "ctx", "head"),
        P("grp", "ctx", "head"),
        P("grp", "ctx", "head"),
        P("grp", None, None),
        P("grp", None),
        P("grp", None),
    )
    chain = mesh.shape["ctx"] == SPAN == 4 and mesh.shape["grp"] == 2
    local = chain_local if chain else ring_local
    out_specs = P("grp", "ctx", "head")
    return jax.shard_map(local, mesh=mesh, in_specs=in_specs, out_specs=out_specs, check_vma=False)
```

```python
import functools
import math

import jax
import jax.numpy as jnp
from jax import lax
from jax.experimental import pallas as pl
from jax.experimental.pallas import tpu as pltpu
from jax.sharding import PartitionSpec as P


HD = 128
SPAN = 4
PAGE = 64
CAP = 6


neg_floor = -1e30
far_limit = 1 << 30
log2_scale = math.log2(math.e) / math.sqrt(HD)

HBM = pl.BlockSpec(memory_space=pltpu.HBM)
VMEM = pl.BlockSpec(memory_space=pltpu.VMEM)
SMEM = pl.BlockSpec(memory_space=pltpu.SMEM)


def call(body, outs, in_specs, out_specs, scratch=(), flops=0, nbytes=0):
    return pl.pallas_call(
        body,
        out_shape=outs,
        in_specs=in_specs,
        out_specs=out_specs,
        scratch_shapes=scratch,
        compiler_params=pltpu.CompilerParams(vmem_limit_bytes=40 << 20),
        cost_estimate=pl.CostEstimate(flops=flops, bytes_accessed=nbytes, transcendentals=0),
    )


def sds(shape, dtype=jnp.bfloat16):
    return jax.ShapeDtypeStruct(shape, dtype)


def listed_pages(tables, places, limits, source, most, sem):
    table, slot, length = places
    holders = lax.axis_size("ctx")
    held = slot.shape[1] // holders
    reads = [
        pltpu.make_async_copy(wide, near, sem.at[i])
        for i, (wide, near) in enumerate(zip(tables, places))
    ]
    for copy in reads:
        copy.start()
    for i in range(holders * held):
        limits[i] = 0
        source[i] = 0
    for copy in reads:
        copy.wait()
    counts = [jnp.int32(0)] * holders
    for i in range(table.shape[2]):
        number = table[0, 0, i]
        place = slot[0, number]
        holder = lax.div(place, jnp.int32(held))
        nth = counts[-1]
        for h in range(holders - 1):
            nth = jnp.where(holder == h, counts[h], nth)
        counts = [c + (holder == h).astype(jnp.int32) for h, c in enumerate(counts)]
        limits[holder * held + nth] = length[0, number]
        source[holder * held + nth] = place - holder * held
    for i in range(holders):
        limits[holders * held + i] = counts[i]
    most[0] = functools.reduce(jnp.maximum, counts)


def page_copies(packs, pages, source, first, cap, sem):
    position = lax.axis_index("ctx")
    held = source.shape[0] // lax.axis_size("ctx")
    copies = []
    for g, pack in enumerate(packs):
        for j in range(cap):
            row = pl.multiple_of(source[position * held + first + j] * PAGE, PAGE)
            for w, wide in enumerate(pages):
                copy = pltpu.make_async_copy(
                    wide.at[0, pl.ds(row, PAGE), pl.ds(g * HD, HD)],
                    pack.at[w, pl.ds(j * PAGE, PAGE), :],
                    sem.at[(j * 2 + g) * 2 + w],
                )
                copy.start()
                copies.append(copy)
    return copies


def pack_body(
    table_in, slot_in, length_in, pk, pv, nk, nv, pack0, pack1, fresh, limits, most,
    table, slot, length, source, sem, sem_new, *, cap
):
    rows_dev = nk.shape[1]
    copies = []
    for w, new in enumerate((nk, nv)):
        for g in range(2):
            for n, (pack, row) in enumerate(((pack0, cap * PAGE), (fresh, 0))):
                copies.append(
                    pltpu.make_async_copy(
                        new.at[0, :, pl.ds(g * HD, HD)],
                        pack.at[w, pl.ds(row + g * rows_dev, rows_dev), :],
                        sem_new.at[(n * 2 + w) * 2 + g],
                    )
                )
    for copy in copies:
        copy.start()
    listed_pages(
        (table_in, slot_in, length_in), (table, slot, length), limits, source, most, sem
    )
    copies += page_copies((pack0, pack1), (pk, pv), source, 0, cap, sem)
    for copy in copies:
        copy.wait()


def spare_body(
    table_in, slot_in, length_in, pk, pv, rest, table, slot, length, source, limits, most,
    sem, *, first, cap
):
    listed_pages(
        (table_in, slot_in, length_in), (table, slot, length), limits, source, most, sem
    )
    for copy in page_copies((rest.at[0], rest.at[1]), (pk, pv), source, first, cap, sem):
        copy.wait()


def blank_body(*refs):
    pass


def holder_ids(position):
    left = position < 2
    return (
        position,
        position ^ 1,
        jnp.where(left, 2, 1),
        jnp.where(left, 3, 0),
    )


def is_inner(position):
    return (position == 1) | (position == 2)


def heads_of(ref, g):
    group = ref.shape[2] // HD // 2
    return jnp.concatenate(
        [ref[0, :, i * HD : (i + 1) * HD] for i in range(g * group, (g + 1) * group)], axis=0
    )


def page_bias(limits, first, count):
    column = lax.broadcasted_iota(jnp.int32, (1, count * PAGE), 1)
    page = column // PAGE
    within = column - page * PAGE
    limit = jnp.zeros((1, count * PAGE), jnp.int32)
    for j in range(count):
        limit = jnp.where(page == j, limits[first + j], limit)
    return jnp.where(within < limit, 0.0, neg_floor).astype(jnp.float32)


def held_pages(limits):
    holders = lax.axis_size("ctx")
    return limits.shape[0] // holders - 1


def join_limits(limits, ids, cap, joined):
    holders = lax.axis_size("ctx")
    held = held_pages(limits)
    for i in range(joined.shape[0]):
        joined[i] = 0
    offsets = []
    offset = jnp.int32(0)
    for holder in ids:
        offsets.append(offset)
        for j in range(cap):
            joined[offset + j] = limits[holder * held + j]
        offset = offset + jnp.minimum(limits[holders * held + holder], cap)
    return offsets, offset


def plan_body(limits, marks, bias_early, bias_late, bias_spare, joined, last, *, cap, early):
    holders = lax.axis_size("ctx")
    held = held_pages(limits)
    ids = holder_ids(lax.axis_index("ctx"))
    offsets, total = join_limits(limits, ids[:3], cap, joined)
    more = jnp.maximum(total - early, 0)
    for j in range(cap):
        last[j] = joined[early + j]
    for j in range(cap):
        last[more + j] = limits[ids[3] * held + j]
    most = functools.reduce(jnp.maximum, [limits[holders * held + i] for i in range(holders)])
    for i, mark in enumerate((offsets[1], offsets[2], more, most)):
        marks[i] = mark
    for ref, bias in (
        (bias_early, page_bias(joined, 0, early)),
        (bias_late, page_bias(last, 0, cap)),
    ):
        ref[...] = jnp.broadcast_to(bias, ref.shape)
    for i, holder in enumerate(ids):
        bias = page_bias(limits, holder * held + cap, held - cap)
        bias_spare[i] = jnp.broadcast_to(bias, bias_spare.shape[1:])


def place_pages(dense, packs, offsets, cap):
    for b, pack in enumerate(packs):
        dense[:, b * cap * PAGE : (b + 1) * cap * PAGE, :] = pack[:, : cap * PAGE, :]
    for pack, offset in list(zip(packs, offsets))[1:]:
        row = pl.multiple_of(offset * PAGE, PAGE)
        dense[:, pl.ds(row, cap * PAGE), :] = pack[:, : cap * PAGE, :]


def causal_bias(position, ids, rows, rows_dev):
    shape = (rows_dev, len(ids) * rows_dev)
    row = lax.broadcasted_iota(jnp.int32, shape, 0)
    column = lax.broadcasted_iota(jnp.int32, (1, shape[1]), 1)
    key = jnp.zeros_like(column)
    for i, holder in enumerate(ids):
        key = jnp.where(column // rows_dev == i, column + (holder - i) * rows_dev, key)
    allowed = position * rows_dev + row >= key
    bias = jnp.where(allowed, 0.0, neg_floor).astype(jnp.float32)
    return jnp.concatenate([bias] * (rows // rows_dev), axis=0)


def scores_of(q, blocks):
    return [
        lax.dot_general(q, k, (((1,), (1,)), ((), ())), preferred_element_type=jnp.float32)
        for k, _, _ in blocks
    ]


def softmax_of(raw, blocks, state=None):
    scores = [s * log2_scale + bias for s, (_, _, bias) in zip(raw, blocks)]
    shape = (raw[0].shape[0], HD)
    top = functools.reduce(jnp.maximum, [jnp.max(s, axis=1, keepdims=True) for s in scores])
    if state is not None:
        old_top, old_total, old_acc = state
        wide = jnp.maximum(jnp.broadcast_to(top, shape), old_top)
        rescale = jnp.exp2(old_top - wide)
        top = wide[:, 0:1]
    total = 0.0
    acc = 0.0
    for s, (_, v, _) in zip(scores, blocks):
        w = jnp.exp2(s - top)
        total = total + jnp.sum(w, axis=1, keepdims=True)
        acc = acc + jnp.dot(w.astype(jnp.bfloat16), v, preferred_element_type=jnp.float32)
    if state is None:
        return top, total, acc
    total = jnp.broadcast_to(total, shape) + old_total * rescale
    return total, acc + old_acc * rescale


def in_turn(units):
    pending = None
    for queries, blocks, use in units:
        raw = scores_of(queries(), blocks)
        if pending is not None:
            pending()
        pending = functools.partial(use, raw, blocks)
    pending()


def early_blocks(marks, bias_early, news, packs, dense, target, rows_dev, rows, g, early, cap):
    ids = holder_ids(lax.axis_index("ctx"))
    split = early * PAGE
    place_pages(dense, packs, (0, marks[0], marks[1]), cap)
    firsts = [n.shape[1] - 2 * rows_dev + g * rows_dev for n in news]
    nk = jnp.concatenate([n[0, i : i + rows_dev] for n, i in zip(news, firsts)], axis=0)
    nv = jnp.concatenate([n[1, i : i + rows_dev] for n, i in zip(news, firsts)], axis=0)
    paged = (dense[0, :split], dense[1, :split], bias_early[0:1, :])
    return [paged, (nk, nv, causal_bias(target, ids, rows, rows_dev))]


def late_blocks(marks, bias_late, taken, left, last, dense, rows_dev, g, cap):
    place_pages(dense, (left, last), (0, marks[2]), cap)
    new = slice(g * rows_dev, (g + 1) * rows_dev)
    shut = jnp.where(lax.axis_index("grp") == 1, 0.0, neg_floor).astype(jnp.float32)
    tk = jnp.concatenate([taken[i, 0, new] for i in range(taken.shape[0])], axis=0)
    tv = jnp.concatenate([taken[i, 1, new] for i in range(taken.shape[0])], axis=0)
    return [
        (dense[0, : cap * PAGE], dense[1, : cap * PAGE], bias_late[0:1, :]),
        (tk, tv, jnp.full((1, tk.shape[0]), shut, jnp.float32)),
    ]


def spare_blocks(bias_spare, spilled, extra, sem, g):
    copies = [
        pltpu.make_async_copy(ref.at[g], extra.at[i], sem.at[i]) for i, ref in enumerate(spilled)
    ]
    for copy in copies:
        copy.start()
    for copy in copies:
        copy.wait()
    return [(extra[i, 0], extra[i, 1], bias_spare[i, 0:1, :]) for i in range(len(spilled))]


def put_heads(out, result, rows_dev):
    for i in range(out.shape[1] // HD):
        out[:, i * HD : (i + 1) * HD] = result[i * rows_dev : (i + 1) * rows_dev]


def when_inner(over, finish):
    inner = is_inner(lax.axis_index("ctx"))

    @pl.when(inner & jnp.logical_not(over))
    def _():
        finish(False)

    @pl.when(inner & over)
    def _():
        finish(True)


def early_body(marks, bias_early, q, *refs, cap, early, g):
    news = refs[:4]
    packs = refs[4:7] if g else news[:3]
    top_out, total_out, acc_out, left, dense = refs[-5:]
    position = lax.axis_index("ctx")
    split = early * PAGE

    @pl.when(is_inner(position))
    def _():
        blocks = early_blocks(
            marks, bias_early, news, packs, dense, position ^ 1, q.shape[1], acc_out.shape[0], g,
            early, cap,
        )
        left[...] = dense[:, split : split + left.shape[1], :]
        top, total, acc = softmax_of(scores_of(heads_of(q, g), blocks), blocks)
        top_out[...] = jnp.broadcast_to(top, acc.shape)
        total_out[...] = jnp.broadcast_to(total, acc.shape)
        acc_out[...] = acc


def late_body(
    marks, bias_late, bias_spare, q, taken, top, total, acc, left, last, s0, s1, s2, s3, out,
    extra, sem, dense, *, cap, g
):
    def finish(more):
        rows_dev = q.shape[1]
        blocks = late_blocks(marks, bias_late, taken, left, last, dense, rows_dev, g, cap)
        if more:
            blocks += spare_blocks(bias_spare, (s0, s1, s2, s3), extra, sem, g)
        raw = scores_of(heads_of(q, g), blocks)
        sums, num = softmax_of(raw, blocks, (top[...], total[...], acc[...]))
        put_heads(out, (num / sums).astype(jnp.bfloat16), rows_dev)

    when_inner(marks[3] > cap, finish)


def full_body(
    marks, bias_early, bias_late, bias_spare, q, taken, *refs, cap, early
):
    news, packs1 = refs[:4], refs[4:7]
    lefts, lasts, spilled = refs[7:9], refs[9:11], refs[11:15]
    outs = refs[15:17]
    extra, sem, dense_early, dense_late = refs[17:]

    def finish(more):
        rows_dev = q.shape[1]
        rows = q.shape[2] // HD // 2 * rows_dev
        position = lax.axis_index("ctx")

        def unit(g):
            packs = packs1 if g else news[:3]
            blocks = early_blocks(
                marks, bias_early, news, packs, dense_early.at[g], position, rows_dev, rows, g,
                early, cap,
            )
            blocks += late_blocks(
                marks, bias_late, taken, lefts[g], lasts[g], dense_late.at[g], rows_dev, g, cap
            )
            if more:
                blocks += spare_blocks(bias_spare, spilled, extra.at[g], sem, g)

            def use(raw, blocks):
                _, sums, num = softmax_of(raw, blocks)
                put_heads(outs[g], (num / sums).astype(jnp.bfloat16), rows_dev)

            return functools.partial(heads_of, q, g), blocks, use

        in_turn(unit(g) for g in range(2))

    when_inner(marks[3] > cap, finish)


def join_body(own0, own1, back0, back1, out):
    inner = is_inner(lax.axis_index("ctx"))
    half = own0.shape[1]

    @pl.when(inner)
    def _():
        out[0, :, :half] = own0[...]
        out[0, :, half:] = own1[...]

    @pl.when(jnp.logical_not(inner))
    def _():
        out[0, :, :half] = back0[...]
        out[0, :, half:] = back1[...]


def chain_local(*args):
    return chain_steps(*args)


def chain_steps(
    queries, new_keys, new_values, page_keys, page_values, page_table, page_slot, page_length
):
    rows_dev = queries.shape[1]
    width = new_keys.shape[2]
    group = queries.shape[2] // width
    holders = lax.axis_size("ctx")
    heads = lax.axis_size("head")
    held = page_slot.shape[1] // holders
    cap = CAP
    keys = cap * PAGE
    side = [(i, i ^ 1) for i in range(holders)]
    middle = []
    for h in range(heads):
        other = h ^ 1 if h ^ 1 < heads else h
        for c in range(holders):
            if c in (1, 2):
                middle.append((c * heads + h, (3 - c) * heads + h))
            else:
                middle.append((c * heads + h, c * heads + other))

    def swap_side(x):
        return lax.ppermute(x, "ctx", side)

    def swap_middle(x):
        return lax.ppermute(x, ("ctx", "head"), middle)

    def from_far_end(x):
        return lax.ppermute(x, "ctx", [(0, 2), (2, 3), (3, 1), (1, 0)])

    def swap_pools(x):
        return lax.ppermute(x, "grp", [(0, 1), (1, 0)])

    new_keys, new_values, page_table, page_slot, page_length, page_keys, page_values = [
        pltpu.with_memory_space_constraint(x, pltpu.HBM)
        for x in (
            new_keys, new_values, page_table, page_slot, page_length, page_keys, page_values,
        )
    ]
    half = sds((rows_dev, group * HD))
    q_end = swap_side(queries)
    tables = (page_table, page_slot, page_length, page_keys, page_values)
    scalars = [
        pltpu.SMEM(page_table.shape, jnp.int32),
        pltpu.SMEM(page_slot.shape, jnp.int32),
        pltpu.SMEM(page_length.shape, jnp.int32),
        pltpu.SMEM((holders * held,), jnp.int32),
    ]
    pack0, pack1, fresh, limits, most = call(
        functools.partial(pack_body, cap=cap),
        (
            sds((2, keys + 2 * rows_dev, HD)),
            sds((2, keys, HD)),
            sds((2, 2 * rows_dev, HD)),
            sds((holders * held + holders,), jnp.int32),
            sds((1,), jnp.int32),
        ),
        [HBM] * 7,
        (VMEM,) * 3 + (SMEM, SMEM),
        scalars + [pltpu.SemaphoreType.DMA((cap * 4,)), pltpu.SemaphoreType.DMA((8,))],
        nbytes=3 << 20,
    )(*tables, new_keys, new_values)

    near0 = swap_side(pack0)
    far0 = swap_middle(pack0)
    n_last = from_far_end(fresh)
    far1 = swap_middle(pack1)
    near1 = swap_side(pack1)
    last0 = swap_middle(near0[:, :keys])
    taken = swap_pools(jnp.stack([fresh, near0[:, keys:], far0[:, keys:], n_last]))
    last1 = swap_middle(near1)
    early_pages = page_table.shape[2] - cap
    marks, bias_early, bias_late, bias_spare = call(
        functools.partial(plan_body, cap=cap, early=early_pages),
        (
            sds((8,), jnp.int32),
            sds((8, early_pages * PAGE), jnp.float32),
            sds((8, keys), jnp.float32),
            sds((holders, 8, (held - cap) * PAGE), jnp.float32),
        ),
        [SMEM],
        (SMEM, VMEM, VMEM, VMEM),
        [pltpu.SMEM((early_pages + 2 * cap,), jnp.int32), pltpu.SMEM((2 * cap,), jnp.int32)],
        nbytes=1 << 19,
    )(limits)
    spare = sds((2, 2, (held - cap) * PAGE, HD))

    def fetch():
        rest = call(
            functools.partial(spare_body, first=cap, cap=held - cap),
            spare,
            [HBM] * 5,
            VMEM,
            scalars
            + [
                pltpu.SMEM((holders * held + holders,), jnp.int32),
                pltpu.SMEM((1,), jnp.int32),
                pltpu.SemaphoreType.DMA((max(held - cap, 1) * 4,)),
            ],
            nbytes=1 << 20,
        )(*tables)
        near = swap_side(rest)
        far = swap_middle(rest)
        return rest, near, far, from_far_end(rest)

    def skip():
        return tuple(call(blank_body, (spare,) * 4, [], (HBM,) * 4)())

    spilled = lax.cond(most[0] > cap, fetch, skip)

    rows = group * rows_dev
    pair_flops = 4 * rows * HD
    news = (pack0, near0, far0, n_last)
    packs1 = (pack1, near1, far1)
    state = (sds((rows, HD), jnp.float32),) * 3
    wide_pages = (2, (early_pages + 2 * cap) * PAGE, HD)
    late_pages = (2, 2 * keys, HD)
    spare_pages = (4, 2, (held - cap) * PAGE, HD)
    lasts = (last0, last1)

    def early(g):
        packs = packs1 if g else ()
        *carried, left = call(
            functools.partial(early_body, cap=cap, early=early_pages, g=g),
            state + (sds((2, keys, HD)),),
            [SMEM] + [VMEM] * (6 + len(packs)),
            (VMEM,) * 4,
            [pltpu.VMEM(wide_pages, jnp.bfloat16)],
            flops=pair_flops * (early_pages * PAGE + 4 * rows_dev),
            nbytes=1 << 20,
        )(marks, bias_early, q_end, *news, *packs)
        return carried, left

    def late(g, carried, left):
        return call(
            functools.partial(late_body, cap=cap, g=g),
            half,
            [SMEM] + [VMEM] * 9 + [HBM] * 4,
            VMEM,
            [
                pltpu.VMEM(spare_pages, jnp.bfloat16),
                pltpu.SemaphoreType.DMA((4,)),
                pltpu.VMEM(late_pages, jnp.bfloat16),
            ],
            flops=pair_flops * (keys + 4 * rows_dev),
            nbytes=1 << 20,
        )(marks, bias_late, bias_spare, q_end, taken, *carried, left, lasts[g], *spilled)

    carried0, left0 = early(0)
    carried1, left1 = early(1)
    back0 = swap_side(late(0, carried0, left0))
    back1 = swap_side(late(1, carried1, left1))
    own0, own1 = call(
        functools.partial(full_body, cap=cap, early=early_pages),
        (half, half),
        [SMEM] + [VMEM] * 16 + [HBM] * 4,
        (VMEM, VMEM),
        [
            pltpu.VMEM((2, *spare_pages), jnp.bfloat16),
            pltpu.SemaphoreType.DMA((4,)),
            pltpu.VMEM((2, *wide_pages), jnp.bfloat16),
            pltpu.VMEM((2, *late_pages), jnp.bfloat16),
        ],
        flops=2 * pair_flops * (page_table.shape[2] * PAGE + 8 * rows_dev),
        nbytes=2 << 20,
    )(
        marks, bias_early, bias_late, bias_spare, queries, taken, *news, *packs1, left0, left1,
        *lasts, *spilled,
    )
    return call(join_body, sds(queries.shape), [VMEM] * 4, VMEM, nbytes=1 << 20)(
        own0, own1, back0, back1
    )


def passed_along(block, axis, distance):
    devices = range(lax.axis_size(axis))
    route = [(i - distance, i) for i in devices if i - distance in devices]
    return lax.ppermute(block, axis, route)


def passed_along_2(block, axis, distance):
    devices = range(lax.axis_size(axis))
    route = [((i - distance) % len(devices), i) for i in devices]
    return lax.ppermute(block, axis, route)


def ring_local(
    queries, new_keys, new_values, page_keys, page_values, page_table, page_slot, page_length
):
    query_rows = queries[0]
    rows_dev = query_rows.shape[0]
    key_width = new_keys.shape[2]
    shared_heads = key_width // HD
    query_count = query_rows.shape[1] // HD
    group_size = query_count // shared_heads
    scaling = 1.0 / math.sqrt(HD)
    position = lax.axis_index("ctx")
    cycle_size = lax.axis_size("ctx")
    pool_index = lax.axis_index("grp")
    request = position // SPAN
    row_ids = position * rows_dev + jnp.arange(rows_dev, dtype=jnp.int32)
    query_heads = query_rows.reshape(rows_dev, shared_heads, group_size, HD).transpose(1, 2, 0, 3)
    pages_total = page_slot.shape[1]
    numbers = jnp.arange(pages_total, dtype=jnp.int32)
    listed = jnp.any(page_table[0][:, :, None] == numbers[None, None, :], axis=1).astype(
        jnp.float32
    )
    own_listed = lax.dynamic_index_in_dim(listed, request, 0, keepdims=False)
    placed = (page_slot[0][:, None] == numbers[None, :]).astype(jnp.float32)
    listed_slot = jnp.dot(own_listed, placed, precision=lax.Precision.HIGHEST)
    length_slot = jnp.dot(
        page_length[0].astype(jnp.float32), placed, precision=lax.Precision.HIGHEST
    )
    offsets = jnp.arange(PAGE, dtype=jnp.int32).astype(jnp.float32)
    page_open = (listed_slot[:, None] > 0.5) & (offsets[None, :] < length_slot[:, None])
    page_limits = jnp.where(page_open, 0, far_limit).astype(jnp.int32).reshape(cycle_size, -1)

    def own_limits(holder):
        same = holder // SPAN == request
        return jnp.where(same, holder * rows_dev + jnp.arange(rows_dev, dtype=jnp.int32), far_limit)

    def taken_limits(holder):
        same = (holder // SPAN == request) & (pool_index == 1)
        return jnp.where(same, jnp.zeros((rows_dev,), jnp.int32), far_limit)

    def absorb_rows(carried, key_rows, value_rows, limits):
        maxima, totals, accumulated = carried
        pieces = key_rows.shape[0]
        key_heads = key_rows.reshape(pieces, shared_heads, HD)
        value_heads = value_rows.reshape(pieces, shared_heads, HD)
        scores = (
            jnp.einsum("kgrd,nkd->kgrn", query_heads, key_heads, preferred_element_type=jnp.float32)
            * scaling
        )
        allowed = row_ids[:, None] >= limits[None, :]
        masked = jnp.where(allowed, scores, neg_floor)
        new_max = jnp.maximum(maxima, jnp.max(masked, axis=-1))
        weights = jnp.where(allowed, jnp.exp(masked - new_max[..., None]), 0.0)
        rescale = jnp.exp(maxima - new_max)
        totals = totals * rescale + jnp.sum(weights, axis=-1)
        product = jnp.einsum(
            "kgrn,nkd->kgrd",
            weights.astype(jnp.bfloat16),
            value_heads,
            preferred_element_type=jnp.float32,
        )
        accumulated = accumulated * rescale[..., None] + product
        return (new_max, totals, accumulated)

    own_pairs = jnp.stack([new_keys[0], new_values[0]])
    taken_pairs = passed_along(own_pairs, "grp", 1)
    page_pairs = jnp.stack([page_keys[0], page_values[0]])
    carried = (
        jnp.full((shared_heads, group_size, rows_dev), neg_floor, jnp.float32),
        jnp.zeros((shared_heads, group_size, rows_dev), jnp.float32),
        jnp.zeros((shared_heads, group_size, rows_dev, HD), jnp.float32),
    )
    moving_rows = jnp.concatenate([page_pairs, own_pairs, taken_pairs], axis=1)

    def block_limits(holder):
        page_part = lax.dynamic_index_in_dim(page_limits, holder, 0, keepdims=False)
        return jnp.concatenate([page_part, own_limits(holder), taken_limits(holder)])

    def advance(stride, state_pair):
        inner, travelling = state_pair
        holder = (position - stride) % cycle_size
        inner = absorb_rows(inner, travelling[0], travelling[1], block_limits(holder))
        travelling = passed_along_2(travelling, "ctx", 1)
        return (inner, travelling)

    carried, moving_rows = lax.fori_loop(0, cycle_size - 1, advance, (carried, moving_rows))
    carried = absorb_rows(
        carried, moving_rows[0], moving_rows[1], block_limits((position + 1) % cycle_size)
    )
    _, totals, accumulated = carried
    attended = accumulated / totals[..., None]
    attended = attended.transpose(2, 0, 1, 3).reshape(rows_dev, query_count * HD)
    return attended.astype(jnp.bfloat16)[None]


def solution(mesh):
    in_specs = (
        P("grp", "ctx", "head"),
        P("grp", "ctx", "head"),
        P("grp", "ctx", "head"),
        P("grp", "ctx", "head"),
        P("grp", "ctx", "head"),
        P("grp", None, None),
        P("grp", None),
        P("grp", None),
    )
    chain = mesh.shape["ctx"] == SPAN == 4 and mesh.shape["grp"] == 2
    local = chain_local if chain else ring_local
    out_specs = P("grp", "ctx", "head")
    return jax.shard_map(local, mesh=mesh, in_specs=in_specs, out_specs=out_specs, check_vma=False)
```
